128 devices in a mesh: tm: 16 (over z_lo, x, core), space: 8 (over y, z_hi).
Axes of the slice: x: 4, y: 4, z: 4 (z_hi: 2, z_lo: 2; z = z_hi * 2 + z_lo), core: 2. Of those that a mesh axis runs over, the one named last changes fastest.
Arguments:
- coarse_guess: float32 [16, 64, 12, 512], P('tm', 'space'), may hold values from -6 to 6
- initial_state: float32 [64, 12, 512], P('space'), may hold values from -6 to 6
- fine_volume: bfloat16 [512, 512], replicated
- coarse_volume: bfloat16 [512, 512], replicated
- lift_matrix: bfloat16 [384, 512], replicated, may hold values from -0.0390625 to 0.0390625
- wave_speed: float32 [12], replicated, may hold values from 0.1 to 0.6
- reaction_rate: float32 [24], replicated, may hold values from 0.05 to 0.5
- species_map: int32 [24, 3], replicated, may hold values from 0 to 11
- neighbour_element: int32 [64, 6], P('space'), may hold values from 0 to 7
- neighbour_rank: int32 [64, 6], P('space'), may hold values from -1 to 1
Outputs:
- iterate: float32 [64, 64, 12, 512], P('tm', 'space')
The draws below stay inside these ranges and needn't reach their ends.
All inputs are finite; a program needn't handle non-finite values.
Results may differ from the reference program's by a relative error of at most 0.025.
Values may be sent and summed in bfloat16 or wider, within the bound.
No kernel may reach another device: no remote copies, remote signals or barrier semaphores. Data moves between devices by JAX's collectives and lax.ppermute only.
A program may use at most 64 MiB of HBM per device.

```python
import math
import jax
import jax.numpy as jnp
from jax import lax

SIDE = 8
NODES = 512
FACE_NODES = 384
VARS = 12
REACTIONS = 24
STRIDE = 4
E_DEV = 8
ELEMS = 64
NT = 64
N_TM = 16
N_SPACE = 8


def operator_draw(key, lower, upper, rough):
    diagonal = jax.random.uniform(jax.random.fold_in(key, 11), (NODES,), jnp.float32, lower, upper)
    return (jnp.diag(diagonal) + rough * (0.15 / math.sqrt(NODES))).astype(jnp.bfloat16)


def draw_fine_volume(key, part):
    inner = jax.random.fold_in(key, 101)
    rough = jax.random.normal(jax.random.fold_in(inner, 3), (NODES, NODES), jnp.float32)
    return operator_draw(inner, 0.45, 0.7, rough)


def draw_coarse_volume(key, part):
    inner = jax.random.fold_in(key, 202)
    rough = jax.random.normal(jax.random.fold_in(inner, 3), (NODES, NODES), jnp.float32)
    return operator_draw(inner, 0.35, 0.6, rough)


def with_ends(array, own_key, least, high):
    longest = array.shape.index(max(array.shape))
    spots = []
    for shift in (0, 1):
        where = [jax.random.randint(jax.random.fold_in(own_key, axis), (), 0, length) for axis, length in enumerate(array.shape)]
        where[longest] = (where[longest] + shift) % array.shape[longest]
        spots.append(tuple(where))
    return array.at[spots[0]].set(least).at[spots[1]].set(high)


def steps_of(rng, extent, shards, low, top_value):
    def one(axis_at, shards_of):
        steps = jax.random.uniform(jax.random.fold_in(jax.random.fold_in(rng, 6), axis_at), (shards_of,), jnp.float32, low / len(shards), top_value / len(shards))
        return jnp.repeat(jnp.exp(steps), extent[axis_at] // shards_of).reshape((-1,) + (1,) * (len(extent) - axis_at - 1))

    level = one(*shards[0])
    for cut in shards[1:]:
        level = level * one(*cut)
    return level


def scatter_about(own_key, extent, scale, most, shards=(), kind=jnp.bfloat16):
    entries = scale * jax.random.normal(own_key, extent, jnp.float32)
    if shards:
        entries = entries * steps_of(own_key, extent, shards, -0.22, 0.18)
    return jnp.clip(entries, -most, most).astype(kind)


def setup_inputs(seed: int = 0) -> dict:
    key_list = jax.random.split(jax.random.key(seed), 11)
    coarse_guess = scatter_about(key_list[0], (N_TM, ELEMS, VARS, NODES), 1.0, 6.0, ((0, 16), (1, 8)), jnp.float32)
    initial_state = scatter_about(key_list[1], (ELEMS, VARS, NODES), 1.0, 6.0, ((0, 8),), jnp.float32)
    fine_volume = draw_fine_volume(jax.random.fold_in(key_list[10], 71), 0)
    coarse_volume = draw_coarse_volume(jax.random.fold_in(key_list[10], 71), 0)
    lift_matrix = scatter_about(key_list[4], (FACE_NODES, NODES), (64 * FACE_NODES) ** -0.5, 0.0390625)
    wave_speed = jnp.clip(jnp.exp(jax.random.uniform(key_list[5], (VARS,), jnp.float32, math.log(0.1), math.log(0.6))), 0.1, 0.6)
    reaction_rate = jnp.clip(jnp.exp(jax.random.uniform(key_list[6], (REACTIONS,), jnp.float32, math.log(0.05), math.log(0.5))), 0.05, 0.5)
    species_map = with_ends(jax.random.randint(key_list[7], (REACTIONS, 3), 0, VARS), jax.random.fold_in(key_list[7], 1), 0, VARS - 1).astype(jnp.int32)
    neighbour_element = with_ends(jax.random.randint(key_list[8], (ELEMS, 6), 0, E_DEV), jax.random.fold_in(key_list[8], 1), 0, E_DEV - 1).astype(jnp.int32)
    neighbour_rank = with_ends(jax.random.randint(key_list[9], (ELEMS, 6), -1, 2), jax.random.fold_in(key_list[9], 1), -1, 1).astype(jnp.int32)
    return dict(coarse_guess=coarse_guess, initial_state=initial_state, fine_volume=fine_volume, coarse_volume=coarse_volume, lift_matrix=lift_matrix, wave_speed=wave_speed, reaction_rate=reaction_rate, species_map=species_map, neighbour_element=neighbour_element, neighbour_rank=neighbour_rank)


coarse_gain = 4.0


def face_cut(rounded):
    blocked = rounded.reshape(rounded.shape[:-1] + (SIDE, SIDE, SIDE))
    planes = [blocked[..., 0, :, :], blocked[..., -1, :, :], blocked[..., :, 0, :],
              blocked[..., :, -1, :], blocked[..., :, :, 0], blocked[..., :, :, -1]]
    return jnp.stack([plane.reshape(rounded.shape[:-1] + (SIDE * SIDE,)) for plane in planes], axis=-2)


def selections(species_map):
    labels = jnp.arange(VARS, dtype=jnp.int32)[None, :]
    first_table = (species_map[:, 0:1] == labels).astype(jnp.float32)
    second_table = (species_map[:, 1:2] == labels).astype(jnp.float32)
    made_table = (species_map[:, 2:3] == labels).astype(jnp.float32)
    return first_table, second_table, made_table - first_table


def react(state, tables, scaled_rates):
    first_table, second_table, change_table = tables
    first_amount = jnp.einsum('rv,...vn->...rn', first_table, state, precision=lax.Precision.HIGHEST)
    second_amount = jnp.einsum('rv,...vn->...rn', second_table, state, precision=lax.Precision.HIGHEST)
    speed_term = scaled_rates[:, None] * first_amount * second_amount / (
        1.0 + first_amount * first_amount + second_amount * second_amount)
    return state + jnp.einsum('rv,...rn->...vn', change_table, speed_term, precision=lax.Precision.HIGHEST)


def reference(coarse_guess, initial_state, fine_volume, coarse_volume, lift_matrix, wave_speed,
              reaction_rate, species_map, neighbour_element, neighbour_rank):
    tables = selections(species_map)
    home_block = (jnp.arange(ELEMS, dtype=jnp.int32) // E_DEV)[:, None]
    partner = (((home_block + neighbour_rank) % N_SPACE) * E_DEV + neighbour_element).astype(jnp.int32)

    def substep(state, volume, gain):
        rounded = state.astype(jnp.bfloat16)
        own_faces = face_cut(rounded)
        across = jnp.stack([jnp.take(own_faces[..., which_face ^ 1, :], partner[:, which_face], axis=-3)
                            for which_face in range(6)], axis=-2)
        jumps = (wave_speed[:, None, None] * (across.astype(jnp.float32) - own_faces.astype(jnp.float32)))
        jumps = jumps.astype(jnp.bfloat16).reshape(state.shape[:-1] + (FACE_NODES,))
        moved = jnp.dot(rounded, volume, preferred_element_type=jnp.float32)
        moved = moved + jnp.dot(jumps, lift_matrix, preferred_element_type=jnp.float32)
        return react(moved, tables, reaction_rate * gain)

    def fine_step(state):
        return substep(substep(state, fine_volume, 1.0), fine_volume, 1.0)

    def coarse_step(state):
        return substep(state, coarse_volume, coarse_gain)

    def relax(starts):
        points = []
        current = starts
        for number in range(STRIDE - 1):
            current = fine_step(current)
            points.append(current)
        return points

    starts = jnp.concatenate([initial_state[None], coarse_guess[1:]], axis=0)
    relaxed = fine_step(relax(starts)[-1])
    second = jnp.concatenate([initial_state[None], relaxed[:-1]], axis=0)
    correction = fine_step(relax(second)[-1]) - coarse_step(second)

    def chain(value, term):
        updated = coarse_step(value) + term
        return updated, updated

    final_value, coarse_values = lax.scan(chain, initial_state, correction)
    third = jnp.concatenate([initial_state[None], coarse_values[:-1]], axis=0)
    points = relax(third) + [coarse_values]
    stacked = jnp.stack(points, axis=1)
    return stacked.reshape((NT, ELEMS, VARS, NODES))
```

```python
import jax
import jax.numpy as jnp
import numpy as np
from jax import lax
from jax.experimental import pallas as pl
from jax.experimental.pallas import tpu as pltpu
from jax.sharding import PartitionSpec as P

SIDE = 8
NODES = 512
FACES = 384
VARS = 12
REACTIONS = 24
BLOCK = 8
BLOCKS = 8
ELEMS = 64
ROWS = VARS * ELEMS
OWN = 4
STRIDE = 4
GAIN = 4.0
BF = jnp.bfloat16
F32 = jnp.float32


def swapped_face_table():
    inner = np.arange(64)
    first, second = inner // 8, inner % 8
    nodes = [
        first * 64 + second,
        first * 64 + 56 + second,
        first * 64 + second * 8,
        first * 64 + second * 8 + 7,
    ]
    table = np.zeros((NODES, 256), np.float32)
    for place, face in enumerate((1, 0, 3, 2)):
        table[nodes[face], place * 64 + inner] = 1.0
    return table


def gather_tables(code, table_ref):
    row = lax.broadcasted_iota(jnp.int32, (ELEMS, ELEMS), 0)
    column = lax.broadcasted_iota(jnp.int32, (ELEMS, ELEMS), 1)
    minus = jnp.where(row == column, -1.0, 0.0)
    home = row - jnp.bitwise_and(row, 7)
    for pair in range(3):
        parts = []
        for face in (2 * pair, 2 * pair + 1):
            source = jnp.bitwise_and(home + code[:, face : face + 1] + 56, 63)
            parts.append(jnp.where(source == column, 1.0, 0.0))
        table_ref[pair, :, 0:128] = jnp.concatenate(parts, axis=1).astype(BF)
        table_ref[pair, :, 128:192] = minus.astype(BF)


def transport(xj_ref, t_ref, s_ref, table_ref, face_ref, w_ref, speed_ref):
    lane = lax.broadcasted_iota(jnp.int32, (ELEMS, 128), 1)
    left = lane < 64
    zero = jnp.zeros((ELEMS, 128), BF)
    s_ref[:, 128:384] = jnp.dot(xj_ref[:, 0:NODES], face_ref[...], preferred_element_type=F32).astype(BF)
    lo = xj_ref[:, 0:128]
    hi = xj_ref[:, NODES - 128 : NODES]
    s_ref[:, 0:128] = jnp.concatenate([hi[:, 64:128], lo[:, 0:64]], axis=1)

    for v in range(0, VARS, 2):
        for pair in range(3):
            stacks = []
            for half in range(2):
                swapped = s_ref[pl.ds((v + half) * ELEMS, ELEMS), pair * 128 : (pair + 1) * 128]
                own = jnp.concatenate([swapped[:, 64:128], swapped[:, 0:64]], axis=1)
                stacks.append(
                    jnp.concatenate(
                        [jnp.where(left, swapped, zero), jnp.where(left, zero, swapped), own], axis=0
                    )
                )
            jump = jnp.dot(
                table_ref[pair], jnp.concatenate(stacks, axis=1), preferred_element_type=F32
            )
            for half in range(2):
                xj_ref[pl.ds((v + half) * ELEMS, ELEMS), NODES + pair * 128 : NODES + (pair + 1) * 128] = (
                    jump[:, half * 128 : (half + 1) * 128] * speed_ref[v + half]
                ).astype(BF)

    for cut in range(2):
        lanes = pl.ds(cut * 256, 256)
        moved = jnp.dot(xj_ref[...], w_ref[:, lanes], preferred_element_type=F32)
        t_ref[:, :, lanes] = moved.reshape(VARS, ELEMS, 256).astype(t_ref.dtype)


def react(t_ref, plus_ref, minus_ref, species_ref, rate_ref, gain):
    plus_ref[...] = t_ref[...]
    minus_ref[...] = jnp.zeros_like(minus_ref)

    def one(r, carry):
        first = species_ref[r, 0]
        second = species_ref[r, 1]
        made = species_ref[r, 2]
        a = t_ref[first]
        b = t_ref[second]
        rate = (gain * rate_ref[r]) * (a * b) / (1.0 + a * a + b * b)
        plus_ref[made] += rate
        minus_ref[first] += rate
        return carry

    lax.fori_loop(0, REACTIONS, one, 0)


def substep(xj_ref, t_ref, s_ref, table_ref, face_ref, w_ref, speed_ref,
            plus_ref, minus_ref, species_ref, rate_ref, gain):
    transport(xj_ref, t_ref, s_ref, table_ref, face_ref, w_ref, speed_ref)
    react(t_ref, plus_ref, minus_ref, species_ref, rate_ref, gain)


def state_of(plus_ref, minus_ref):
    return (plus_ref[...] - minus_ref[...]).reshape(ROWS, NODES)


def own_rows(value, v):
    return value[v * ELEMS + OWN * BLOCK : v * ELEMS + (OWN + 1) * BLOCK]


def relax_kernel(group_ref, species_ref, rate_ref, speed_ref, *refs):
    parts = refs[:BLOCKS]
    face_ref, fine_ref, coarse_ref, lift_ref = refs[BLOCKS : BLOCKS + 4]
    send_ref, base_ref, second_ref, table_ref = refs[BLOCKS + 4 : BLOCKS + 8]
    xj, t, s, plus, minus, w, g = refs[BLOCKS + 8 :]
    group = group_ref[0]
    values = [part[...].astype(F32) for part in parts]
    for v in range(VARS):
        rows = jnp.concatenate([p[v * BLOCK : (v + 1) * BLOCK] for p in values], axis=0)
        xj[v * ELEMS : (v + 1) * ELEMS, 0:NODES] = rows.astype(BF)
    codes = jnp.concatenate([p[VARS * BLOCK : (VARS + 1) * BLOCK, 0:128] for p in values], axis=0)
    gather_tables(codes.astype(jnp.int32), table_ref)
    w[0:NODES, :] = fine_ref[...]
    w[NODES:, :] = lift_ref[...]
    second_ref[...] = xj[:, 0:NODES]

    def fine(index, carry):
        substep(xj, t, s, table_ref, face_ref, w, speed_ref, plus, minus, species_ref, rate_ref, 1.0)
        xj[:, 0:NODES] = state_of(plus, minus).astype(BF)
        return carry

    lax.fori_loop(0, 8, fine, 0)

    @pl.when(group == 0)
    def _():
        xj[:, 0:NODES] = second_ref[...]

    second_ref[...] = xj[:, 0:NODES]
    w[0:NODES, :] = coarse_ref[...]
    substep(xj, t, s, table_ref, face_ref, w, speed_ref, plus, minus, species_ref, rate_ref, GAIN)
    g[...] = state_of(plus, minus)
    w[0:NODES, :] = fine_ref[...]
    lax.fori_loop(0, 8, fine, 0)
    last = state_of(plus, minus)
    correction = last - g[...]
    send = jnp.where(group == 1, last, correction)
    send_ref[...] = send.astype(BF)
    base = jnp.where(group <= 1, last, correction)
    for v in range(VARS):
        base_ref[v] = own_rows(base, v)


def chain_kernel(group_ref, species_ref, rate_ref, speed_ref,
                 first_ref, term_ref, second_ref, base_ref, table_ref,
                 face_ref, fine_ref, coarse_ref, lift_ref, out_ref,
                 xj, t, s, plus, minus, w, begin):
    group = group_ref[0]
    step = pl.program_id(0)
    index = step + 2

    @pl.when(step == 0)
    def _():
        w[0:NODES, :] = coarse_ref[...]
        w[NODES:, :] = lift_ref[...]
        xj[:, 0:NODES] = first_ref[0]
        begin[...] = second_ref[...]
        out_ref[STRIDE - 1] = base_ref[...]

    @pl.when(index == group)
    def _():
        begin[...] = xj[:, 0:NODES]

    substep(xj, t, s, table_ref, face_ref, w, speed_ref, plus, minus, species_ref, rate_ref, GAIN)
    stepped = state_of(plus, minus)

    @pl.when(index == group)
    def _():
        for v in range(VARS):
            out_ref[STRIDE - 1, v] = own_rows(stepped, v) + base_ref[v]

    xj[:, 0:NODES] = (stepped + term_ref[0].astype(F32)).astype(BF)

    @pl.when(step == pl.num_programs(0) - 1)
    def _():
        w[0:NODES, :] = fine_ref[...]
        xj[:, 0:NODES] = begin[...]

        def fine(index, carry):
            substep(
                xj, t, s, table_ref, face_ref, w, speed_ref, plus, minus, species_ref, rate_ref, 1.0
            )
            state = state_of(plus, minus)
            xj[:, 0:NODES] = state.astype(BF)
            for v in range(VARS):
                out_ref[index // 2, v] = own_rows(state, v)
            return carry

        lax.fori_loop(0, 2 * (STRIDE - 1), fine, 0)


VMEM_SPEC = pl.BlockSpec(memory_space=pltpu.VMEM)
SMEM_SPEC = pl.BlockSpec(memory_space=pltpu.SMEM)


def work_buffers():
    return [
        pltpu.VMEM((ROWS, NODES + FACES), BF),
        pltpu.VMEM((VARS, ELEMS, NODES), F32),
        pltpu.VMEM((ROWS, FACES), BF),
        pltpu.VMEM((VARS, ELEMS, NODES), F32),
        pltpu.VMEM((VARS, ELEMS, NODES), F32),
        pltpu.VMEM((NODES + FACES, NODES), BF),
    ]


def body(
    coarse_guess,
    initial_state,
    fine_volume,
    coarse_volume,
    lift_matrix,
    wave_speed,
    reaction_rate,
    species_map,
    neighbour_element,
    neighbour_rank,
):
    group = lax.axis_index("tm")
    groups = lax.axis_size("tm")
    start = jnp.where((group == 0) | (group == groups - 1), initial_state, coarse_guess[0])
    start = jnp.transpose(start, (1, 0, 2)).reshape(VARS * BLOCK, NODES).astype(BF)
    code = ((neighbour_rank + 1) * BLOCK + neighbour_element).astype(BF)
    code = jnp.pad(code, ((0, 8), (0, NODES - 6)))
    payload = jnp.concatenate([start, code], axis=0)
    parts = []
    for place in range(BLOCKS):
        pairs = []
        for source in range(groups):
            for block in range(BLOCKS):
                target = (source + 1) % groups
                pairs.append((source * BLOCKS + block, target * BLOCKS + (block + OWN - place) % BLOCKS))
        parts.append(lax.ppermute(payload, ("tm", "space"), pairs))
    face_table = jnp.asarray(swapped_face_table()).astype(BF)
    group_array = group.astype(jnp.int32).reshape(1)
    params = pltpu.CompilerParams(vmem_limit_bytes=56 * 1024 * 1024)
    send, base, second, table = pl.pallas_call(
        relax_kernel,
        out_shape=(
            jax.ShapeDtypeStruct((ROWS, NODES), BF),
            jax.ShapeDtypeStruct((VARS, BLOCK, NODES), F32),
            jax.ShapeDtypeStruct((ROWS, NODES), BF),
            jax.ShapeDtypeStruct((3, ELEMS, 192), BF),
        ),
        in_specs=[SMEM_SPEC] * 4 + [VMEM_SPEC] * (BLOCKS + 4),
        out_specs=(VMEM_SPEC,) * 4,
        scratch_shapes=work_buffers() + [pltpu.VMEM((ROWS, NODES), F32)],
        compiler_params=params,
    )(
        group_array, species_map, reaction_rate, wave_speed,
        *parts, face_table, fine_volume, coarse_volume, lift_matrix,
    )
    terms = lax.all_gather(send, "tm", axis=0, tiled=False)
    full = lambda *shape: pl.BlockSpec(shape, lambda k: (0,) * len(shape))
    out = pl.pallas_call(
        chain_kernel,
        grid=(14,),
        out_shape=jax.ShapeDtypeStruct((STRIDE, VARS, BLOCK, NODES), F32),
        in_specs=[SMEM_SPEC] * 4
        + [
            pl.BlockSpec((1, ROWS, NODES), lambda k: (1, 0, 0)),
            pl.BlockSpec((1, ROWS, NODES), lambda k: (k + 2, 0, 0)),
            full(ROWS, NODES),
            full(VARS, BLOCK, NODES),
            full(3, ELEMS, 192),
            full(NODES, 256),
            full(NODES, NODES),
            full(NODES, NODES),
            full(FACES, NODES),
        ],
        out_specs=full(STRIDE, VARS, BLOCK, NODES),
        scratch_shapes=work_buffers() + [pltpu.VMEM((ROWS, NODES), BF)],
        compiler_params=params,
    )(
        group_array, species_map, reaction_rate, wave_speed,
        terms, terms, second, base, table, face_table, fine_volume, coarse_volume, lift_matrix,
    )
    return jnp.transpose(out, (0, 2, 1, 3))


def solution(mesh):
    placed = (
        P("tm", "space", None, None),
        P("space", None, None),
        P(),
        P(),
        P(),
        P(),
        P(),
        P(),
        P("space", None),
        P("space", None),
    )
    return jax.shard_map(
        body, mesh=mesh, in_specs=placed, out_specs=P("tm", "space", None, None), check_vma=False
    )
```

```python
import jax
import jax.numpy as jnp
import numpy as np
from jax import lax
from jax.experimental import pallas as pl
from jax.experimental.pallas import tpu as pltpu
from jax.sharding import PartitionSpec as P

SIDE = 8
NODES = 512
FACES = 384
VARS = 12
REACTIONS = 24
BLOCK = 8
BLOCKS = 8
ELEMS = 64
ROWS = VARS * ELEMS
HALF = NODES // 2
OWN = 4
STRIDE = 4
GAIN = 4.0
BF = jnp.bfloat16
F32 = jnp.float32


def swapped_face_table():
    inner = np.arange(64)
    first, second = inner // 8, inner % 8
    nodes = [
        first * 64 + second,
        first * 64 + 56 + second,
        first * 64 + second * 8,
        first * 64 + second * 8 + 7,
    ]
    table = np.zeros((NODES, 256), np.float32)
    for place, face in enumerate((1, 0, 3, 2)):
        table[nodes[face], place * 64 + inner] = 1.0
    return table


def gather_tables(code, table_ref):
    row = lax.broadcasted_iota(jnp.int32, (ELEMS, ELEMS), 0)
    column = lax.broadcasted_iota(jnp.int32, (ELEMS, ELEMS), 1)
    home = row - jnp.bitwise_and(row, 7)
    for pair in range(3):
        parts = []
        for face in (2 * pair, 2 * pair + 1):
            source = jnp.bitwise_and(home + code[:, face : face + 1] + 56, 63)
            parts.append(jnp.where(source == column, 1.0, 0.0))
        table_ref[pair] = jnp.concatenate(parts, axis=1).astype(BF)


def exchange(xj_ref, s_ref, table_ref, face_ref, speed_ref):
    lane = lax.broadcasted_iota(jnp.int32, (ELEMS, 128), 1)
    left = lane < 64
    zero = jnp.zeros((ELEMS, 128), BF)
    s_ref[:, 128:384] = jnp.dot(
        xj_ref[:, 0:NODES], face_ref[...], preferred_element_type=F32
    ).astype(BF)
    lo = xj_ref[:, 0:128]
    hi = xj_ref[:, NODES - 128 : NODES]
    s_ref[:, 0:128] = jnp.concatenate([hi[:, 64:128], lo[:, 0:64]], axis=1)
    for v in range(0, VARS, 2):
        for pair in range(3):
            lanes = slice(pair * 128, (pair + 1) * 128)
            stacks = []
            for half in range(2):
                swapped = s_ref[(v + half) * ELEMS : (v + half + 1) * ELEMS, lanes]
                stacks.append(
                    jnp.concatenate(
                        [jnp.where(left, swapped, zero), jnp.where(left, zero, swapped)], axis=0
                    )
                )
            across = jnp.dot(
                table_ref[pair], jnp.concatenate(stacks, axis=1), preferred_element_type=F32
            )
            for half in range(2):
                rows = slice((v + half) * ELEMS, (v + half + 1) * ELEMS)
                swapped = s_ref[rows, lanes]
                own = jnp.concatenate([swapped[:, 64:128], swapped[:, 0:64]], axis=1).astype(F32)
                xj_ref[rows, NODES + pair * 128 : NODES + (pair + 1) * 128] = (
                    (across[:, half * 128 : (half + 1) * 128] - own) * speed_ref[v + half]
                ).astype(BF)


def move(xj_ref, w_ref, t_ref, cut, row, rows):
    moved = jnp.dot(
        xj_ref[row : row + rows, :],
        w_ref[:, cut * HALF : (cut + 1) * HALF],
        preferred_element_type=F32,
    )
    t_ref[row // ELEMS : (row + rows) // ELEMS] = moved.reshape(rows // ELEMS, ELEMS, HALF)


def prepare(work, cut):
    t = work.t[cut][...]
    work.plus[cut][...] = t
    work.square[cut][...] = 0.5 + t * t
    work.minus[cut][...] = jnp.zeros_like(t)


def react(work, cut, reaction):
    first, second, made, scale = reaction
    t, square = work.t[cut], work.square[cut]
    rate = scale * (t[first] * t[second]) / (square[first] + square[second])
    work.plus[cut][made] += rate
    work.minus[cut][first] += rate


def result(work, cut):
    return work.plus[cut][...] - work.minus[cut][...]


def own_result(work, cut):
    rows = slice(OWN * BLOCK, (OWN + 1) * BLOCK)
    return work.plus[cut][:, rows, :] - work.minus[cut][:, rows, :]


def substep(work, reactions, finish):
    exchange(work.xj, work.s, work.table, work.face, work.speed)
    move(work.xj, work.w, work.t[0], 0, 0, ROWS)
    prepare(work, 0)
    for number, reaction in enumerate(reactions):
        react(work, 0, reaction)
        if number % 4 == 1:
            move(work.xj, work.w, work.t[1], 1, number // 4 * 128, 128)
    finish(0)
    prepare(work, 1)
    for reaction in reactions:
        react(work, 1, reaction)
    finish(1)


def reactions_of(species_ref, rate_ref, gain):
    return [
        (species_ref[r, 0], species_ref[r, 1], species_ref[r, 2], gain * rate_ref[r])
        for r in range(REACTIONS)
    ]


def half(cut):
    return slice(cut * HALF, (cut + 1) * HALF)


def keep(work):
    def finish(cut):
        work.xj[:, half(cut)] = result(work, cut).astype(BF).reshape(ROWS, HALF)

    return finish


def relax_kernel(group_ref, species_ref, rate_ref, speed_ref, *refs):
    parts = refs[:BLOCKS]
    face_ref, fine_ref, coarse_ref, lift_ref = refs[BLOCKS : BLOCKS + 4]
    send_ref, base_ref, second_ref, table_ref = refs[BLOCKS + 4 : BLOCKS + 8]
    work = Work(refs[BLOCKS + 8 : -2], table_ref, face_ref, speed_ref)
    stepped = refs[-2:]
    xj, w = work.xj, work.w
    group = group_ref[0]
    values = [part[...].astype(F32) for part in parts]
    for v in range(VARS):
        rows = jnp.concatenate([p[v * BLOCK : (v + 1) * BLOCK] for p in values], axis=0)
        xj[v * ELEMS : (v + 1) * ELEMS, 0:NODES] = rows.astype(BF)
    codes = jnp.concatenate([p[VARS * BLOCK : (VARS + 1) * BLOCK, 0:128] for p in values], axis=0)
    gather_tables(codes.astype(jnp.int32), table_ref)
    w[0:NODES, :] = fine_ref[...]
    w[NODES:, :] = lift_ref[...]
    second_ref[...] = xj[:, 0:NODES]
    reactions = reactions_of(species_ref, rate_ref, 1.0)

    def fine(index, carry):
        substep(work, reactions, keep(work))
        return carry

    lax.fori_loop(0, 8, fine, 0)

    @pl.when(group == 0)
    def _():
        xj[:, 0:NODES] = second_ref[...]

    second_ref[...] = xj[:, 0:NODES]
    w[0:NODES, :] = coarse_ref[...]

    def hold(cut):
        stepped[cut][...] = result(work, cut)

    substep(work, reactions_of(species_ref, rate_ref, GAIN), hold)
    w[0:NODES, :] = fine_ref[...]
    lax.fori_loop(0, 8, fine, 0)
    own = slice(OWN * BLOCK, (OWN + 1) * BLOCK)
    for cut in range(2):
        last = result(work, cut)
        term = last - stepped[cut][...]
        send_ref[:, half(cut)] = jnp.where(group == 1, last, term).astype(BF).reshape(ROWS, HALF)
        base_ref[:, :, half(cut)] = jnp.where(group <= 1, last[:, own], term[:, own])


def chain_kernel(group_ref, species_ref, rate_ref, speed_ref,
                 first_ref, term_ref, second_ref, base_ref, table_ref,
                 face_ref, fine_ref, coarse_ref, lift_ref, out_ref, *refs):
    work = Work(refs[:-1], table_ref, face_ref, speed_ref)
    begin = refs[-1]
    xj, w = work.xj, work.w
    group = group_ref[0]
    step = pl.program_id(0)
    index = step + 2

    @pl.when(step == 0)
    def _():
        w[0:NODES, :] = coarse_ref[...]
        w[NODES:, :] = lift_ref[...]
        xj[:, 0:NODES] = first_ref[0]
        begin[...] = second_ref[...]
        out_ref[STRIDE - 1] = base_ref[...]

    @pl.when(index == group)
    def _():
        begin[...] = xj[:, 0:NODES]

    def chained(cut):
        value = result(work, cut).reshape(ROWS, HALF) + term_ref[0, :, half(cut)].astype(F32)
        xj[:, half(cut)] = value.astype(BF)

    substep(work, reactions_of(species_ref, rate_ref, GAIN), chained)

    @pl.when(index == group)
    def _():
        for cut in range(2):
            out_ref[STRIDE - 1, :, :, half(cut)] = own_result(work, cut) + base_ref[:, :, half(cut)]

    @pl.when(step == pl.num_programs(0) - 1)
    def _():
        w[0:NODES, :] = fine_ref[...]
        xj[:, 0:NODES] = begin[...]
        reactions = reactions_of(species_ref, rate_ref, 1.0)

        def fine(index, carry):
            substep(work, reactions, keep(work))
            for cut in range(2):
                out_ref[index // 2, :, :, half(cut)] = own_result(work, cut)
            return carry

        lax.fori_loop(0, 2 * (STRIDE - 1), fine, 0)


class Work:
    def __init__(self, refs, table, face, speed):
        self.xj, self.s, self.w = refs[:3]
        self.t, self.plus, self.minus, self.square = (refs[i : i + 2] for i in (3, 5, 7, 9))
        self.table, self.face, self.speed = table, face, speed


VMEM_SPEC = pl.BlockSpec(memory_space=pltpu.VMEM)
SMEM_SPEC = pl.BlockSpec(memory_space=pltpu.SMEM)


def work_buffers():
    return [
        pltpu.VMEM((ROWS, NODES + FACES), BF),
        pltpu.VMEM((ROWS, FACES), BF),
        pltpu.VMEM((NODES + FACES, NODES), BF),
    ] + [pltpu.VMEM((VARS, ELEMS, HALF), F32)] * 8


def body(
    coarse_guess,
    initial_state,
    fine_volume,
    coarse_volume,
    lift_matrix,
    wave_speed,
    reaction_rate,
    species_map,
    neighbour_element,
    neighbour_rank,
):
    group = lax.axis_index("tm")
    groups = lax.axis_size("tm")
    start = jnp.where((group == 0) | (group == groups - 1), initial_state, coarse_guess[0])
    start = jnp.transpose(start, (1, 0, 2)).reshape(VARS * BLOCK, NODES).astype(BF)
    code = ((neighbour_rank + 1) * BLOCK + neighbour_element).astype(BF)
    code = jnp.pad(code, ((0, 8), (0, NODES - 6)))
    payload = jnp.concatenate([start, code], axis=0)
    parts = []
    for place in range(BLOCKS):
        pairs = []
        for source in range(groups):
            for block in range(BLOCKS):
                target = (source + 1) % groups
                pairs.append((source * BLOCKS + block, target * BLOCKS + (block + OWN - place) % BLOCKS))
        parts.append(lax.ppermute(payload, ("tm", "space"), pairs))
    face_table = jnp.asarray(swapped_face_table()).astype(BF)
    group_array = group.astype(jnp.int32).reshape(1)
    params = pltpu.CompilerParams(vmem_limit_bytes=56 * 1024 * 1024)
    send, base, second, table = pl.pallas_call(
        relax_kernel,
        out_shape=(
            jax.ShapeDtypeStruct((ROWS, NODES), BF),
            jax.ShapeDtypeStruct((VARS, BLOCK, NODES), F32),
            jax.ShapeDtypeStruct((ROWS, NODES), BF),
            jax.ShapeDtypeStruct((3, ELEMS, 128), BF),
        ),
        in_specs=[SMEM_SPEC] * 4 + [VMEM_SPEC] * (BLOCKS + 4),
        out_specs=(VMEM_SPEC,) * 4,
        scratch_shapes=work_buffers() + [pltpu.VMEM((VARS, ELEMS, HALF), F32)] * 2,
        compiler_params=params,
    )(
        group_array, species_map, reaction_rate, wave_speed,
        *parts, face_table, fine_volume, coarse_volume, lift_matrix,
    )
    terms = lax.all_gather(send, "tm", axis=0, tiled=False)
    full = lambda *shape: pl.BlockSpec(shape, lambda k: (0,) * len(shape))
    out = pl.pallas_call(
        chain_kernel,
        grid=(14,),
        out_shape=jax.ShapeDtypeStruct((STRIDE, VARS, BLOCK, NODES), F32),
        in_specs=[SMEM_SPEC] * 4
        + [
            pl.BlockSpec((1, ROWS, NODES), lambda k: (1, 0, 0)),
            pl.BlockSpec((1, ROWS, NODES), lambda k: (k + 2, 0, 0)),
            full(ROWS, NODES),
            full(VARS, BLOCK, NODES),
            full(3, ELEMS, 128),
            full(NODES, 256),
            full(NODES, NODES),
            full(NODES, NODES),
            full(FACES, NODES),
        ],
        out_specs=full(STRIDE, VARS, BLOCK, NODES),
        scratch_shapes=work_buffers() + [pltpu.VMEM((ROWS, NODES), BF)],
        compiler_params=params,
    )(
        group_array, species_map, reaction_rate, wave_speed,
        terms, terms, second, base, table, face_table, fine_volume, coarse_volume, lift_matrix,
    )
    return jnp.transpose(out, (0, 2, 1, 3))


def solution(mesh):
    placed = (
        P("tm", "space", None, None),
        P("space", None, None),
        P(),
        P(),
        P(),
        P(),
        P(),
        P(),
        P("space", None),
        P("space", None),
    )
    return jax.shard_map(
        body, mesh=mesh, in_specs=placed, out_specs=P("tm", "space", None, None), check_vma=False
    )
```

```python
import jax
import jax.numpy as jnp
import numpy as np
from jax import lax
from jax.experimental import pallas as pl
from jax.experimental.pallas import tpu as pltpu
from jax.sharding import PartitionSpec as P

SIDE = 8
NODES = 512
FACES = 384
VARS = 12
REACTIONS = 24
BLOCK = 8
BLOCKS = 8
ELEMS = 64
ROWS = VARS * ELEMS
HALF = NODES // 2
PAYLOAD = 112
OWN = 4
STRIDE = 4
GAIN = 4.0
BF = jnp.bfloat16
F32 = jnp.float32


def swapped_face_table():
    inner = np.arange(64)
    first, second = inner // 8, inner % 8
    nodes = [
        first * 64 + second,
        first * 64 + 56 + second,
        first * 64 + second * 8,
        first * 64 + second * 8 + 7,
    ]
    table = np.zeros((NODES, 256), np.float32)
    for place, face in enumerate((1, 0, 3, 2)):
        table[nodes[face], place * 64 + inner] = 1.0
    return table


def gather_tables(code, table_ref):
    row = lax.broadcasted_iota(jnp.int32, (ELEMS, ELEMS), 0)
    column = lax.broadcasted_iota(jnp.int32, (ELEMS, ELEMS), 1)
    home = row - jnp.bitwise_and(row, 7)
    for pair in range(3):
        parts = []
        for face in (2 * pair, 2 * pair + 1):
            source = jnp.bitwise_and(home + code[:, face : face + 1] + 56, 63)
            parts.append(jnp.where(source == column, 1.0, 0.0))
        table_ref[pair] = jnp.concatenate(parts, axis=1).astype(BF)


def exchange(xj_ref, s_ref, table_ref, face_ref, speed_ref, low, high):
    lane = lax.broadcasted_iota(jnp.int32, (ELEMS, 128), 1)
    left = lane < 64
    zero = jnp.zeros((ELEMS, 128), BF)
    s_ref[:, 128:384] = jnp.dot(
        xj_ref[:, 0:NODES], face_ref[...], preferred_element_type=F32
    ).astype(BF)
    lo = xj_ref[:, 0:128]
    hi = xj_ref[:, NODES - 128 : NODES]
    s_ref[:, 0:128] = jnp.concatenate([hi[:, 64:128], lo[:, 0:64]], axis=1)
    for v in range(0, VARS, 2):
        for pair in range(3):
            lanes = slice(pair * 128, (pair + 1) * 128)
            stacks = []
            for half in range(2):
                swapped = s_ref[(v + half) * ELEMS : (v + half + 1) * ELEMS, lanes]
                stacks.append(
                    jnp.concatenate(
                        [jnp.where(left, swapped, zero), jnp.where(left, zero, swapped)], axis=0
                    )
                )
            across = jnp.dot(
                table_ref[pair, low:high], jnp.concatenate(stacks, axis=1), preferred_element_type=F32
            )
            for half in range(2):
                rows = slice((v + half) * ELEMS + low, (v + half) * ELEMS + high)
                swapped = s_ref[rows, lanes]
                own = jnp.concatenate([swapped[:, 64:128], swapped[:, 0:64]], axis=1).astype(F32)
                xj_ref[rows, NODES + pair * 128 : NODES + (pair + 1) * 128] = (
                    (across[:, half * 128 : (half + 1) * 128] - own) * speed_ref[v + half]
                ).astype(BF)


def move(xj_ref, w_ref, t_ref, cut, row, rows):
    moved = jnp.dot(
        xj_ref[row : row + rows, :],
        w_ref[:, cut * HALF : (cut + 1) * HALF],
        preferred_element_type=F32,
    )
    t_ref[row // ELEMS : (row + rows) // ELEMS] = moved.reshape(rows // ELEMS, ELEMS, HALF)


def move_some(xj_ref, w_ref, t_ref, cut, low, high):
    rows = jnp.concatenate([xj_ref[v * ELEMS + low : v * ELEMS + high, :] for v in range(VARS)], axis=0)
    moved = jnp.dot(
        rows, w_ref[:, cut * HALF : (cut + 1) * HALF], preferred_element_type=F32
    )
    t_ref[:, low:high, :] = moved.reshape(VARS, high - low, HALF)


def prepare(work, cut, low, high):
    rows = slice(low, high)
    t = work.t[cut][:, rows, :]
    work.plus[cut][:, rows, :] = t
    work.square[cut][:, rows, :] = 0.5 + t * t
    work.minus[cut][:, rows, :] = jnp.zeros_like(t)


def react(work, cut, reaction, low, high):
    first, second, made, scale = reaction
    rows = slice(low, high)
    t, square = work.t[cut], work.square[cut]
    rate = scale * (t[first, rows] * t[second, rows]) / (square[first, rows] + square[second, rows])
    work.plus[cut][made, rows] += rate
    work.minus[cut][first, rows] += rate


def result(work, cut, low=0, high=ELEMS):
    return work.plus[cut][:, low:high, :] - work.minus[cut][:, low:high, :]


def own_result(work, cut):
    return result(work, cut, OWN * BLOCK, (OWN + 1) * BLOCK)


def substep(work, reactions, finish):
    exchange(work.xj, work.s, work.table, work.face, work.speed, 0, ELEMS)
    move(work.xj, work.w, work.t[0], 0, 0, ROWS)
    prepare(work, 0, 0, ELEMS)
    for number, reaction in enumerate(reactions):
        react(work, 0, reaction, 0, ELEMS)
        if number % 4 == 1:
            move(work.xj, work.w, work.t[1], 1, number // 4 * 128, 128)
    finish(0)
    prepare(work, 1, 0, ELEMS)
    for reaction in reactions:
        react(work, 1, reaction, 0, ELEMS)
    finish(1)


def substep_some(work, reactions, low, high, store):
    exchange(work.xj, work.s, work.table, work.face, work.speed, low, high)
    for cut in range(2):
        move_some(work.xj, work.w, work.t[cut], cut, low, high)
    for cut in range(2):
        prepare(work, cut, low, high)
        for reaction in reactions:
            react(work, cut, reaction, low, high)
        if store:
            value = result(work, cut, low, high).astype(BF)
            for v in range(VARS):
                work.xj[v * ELEMS + low : v * ELEMS + high, half(cut)] = value[v]


def reactions_of(species_ref, rate_ref, gain):
    return [
        (species_ref[r, 0], species_ref[r, 1], species_ref[r, 2], gain * rate_ref[r])
        for r in range(REACTIONS)
    ]


def half(cut):
    return slice(cut * HALF, (cut + 1) * HALF)


def keep(work):
    def finish(cut):
        work.xj[:, half(cut)] = result(work, cut).astype(BF).reshape(ROWS, HALF)

    return finish


def relax_kernel(group_ref, species_ref, rate_ref, speed_ref, *refs):
    pairs = refs[:4]
    face_ref, fine_ref, coarse_ref, lift_ref = refs[4:8]
    send_ref, base_ref, second_ref, table_ref = refs[8:12]
    work = Work(refs[12:-2], table_ref, face_ref, speed_ref)
    stepped = refs[-2:]
    xj, w = work.xj, work.w
    group = group_ref[0]
    even = group_ref[1] == 0
    near = [pair[0:PAYLOAD].astype(F32) for pair in pairs]
    far = [pair[PAYLOAD:].astype(F32) for pair in pairs]
    values = []
    for k in range(4):
        values += [near[k], jnp.where(even, far[k], far[(k + 1) % 4])]
    for v in range(VARS):
        rows = jnp.concatenate([p[v * BLOCK : (v + 1) * BLOCK] for p in values], axis=0)
        xj[v * ELEMS : (v + 1) * ELEMS, 0:NODES] = rows.astype(BF)
    codes = jnp.concatenate([p[VARS * BLOCK : (VARS + 1) * BLOCK, 0:128] for p in values], axis=0)
    gather_tables(codes.astype(jnp.int32), table_ref)
    w[0:NODES, :] = fine_ref[...]
    w[NODES:, :] = lift_ref[...]
    second_ref[...] = xj[:, 0:NODES]
    reactions = reactions_of(species_ref, rate_ref, 1.0)

    def fine(index, carry):
        substep(work, reactions, keep(work))
        return carry

    lax.fori_loop(0, 8, fine, 0)

    @pl.when(group == 0)
    def _():
        xj[:, 0:NODES] = second_ref[...]

    second_ref[...] = xj[:, 0:NODES]
    w[0:NODES, :] = coarse_ref[...]

    def hold(cut):
        stepped[cut][...] = result(work, cut)

    substep(work, reactions_of(species_ref, rate_ref, GAIN), hold)
    w[0:NODES, :] = fine_ref[...]
    lax.fori_loop(0, 8, fine, 0)
    own = slice(OWN * BLOCK, (OWN + 1) * BLOCK)
    for cut in range(2):
        last = result(work, cut)
        term = last - stepped[cut][...]
        send_ref[:, half(cut)] = jnp.where(group == 1, last, term).astype(BF).reshape(ROWS, HALF)
        base_ref[:, :, half(cut)] = jnp.where(group <= 1, last[:, own], term[:, own])


def chain_kernel(group_ref, species_ref, rate_ref, speed_ref,
                 first_ref, term_ref, second_ref, base_ref, table_ref,
                 face_ref, fine_ref, coarse_ref, lift_ref, out_ref, *refs):
    work = Work(refs[:-1], table_ref, face_ref, speed_ref)
    begin = refs[-1]
    xj, w = work.xj, work.w
    group = group_ref[0]
    step = pl.program_id(0)
    index = step + 2

    @pl.when(step == 0)
    def _():
        w[0:NODES, :] = coarse_ref[...]
        w[NODES:, :] = lift_ref[...]
        xj[:, 0:NODES] = first_ref[0]
        begin[...] = second_ref[...]
        out_ref[STRIDE - 1] = base_ref[...]

    @pl.when(index == group)
    def _():
        begin[...] = xj[:, 0:NODES]

    def chained(cut):
        value = result(work, cut).reshape(ROWS, HALF) + term_ref[0, :, half(cut)].astype(F32)
        xj[:, half(cut)] = value.astype(BF)

    substep(work, reactions_of(species_ref, rate_ref, GAIN), chained)

    @pl.when(index == group)
    def _():
        for cut in range(2):
            out_ref[STRIDE - 1, :, :, half(cut)] = own_result(work, cut) + base_ref[:, :, half(cut)]

    @pl.when(step == pl.num_programs(0) - 1)
    def _():
        @pl.when(group == index + 1)
        def _():
            begin[...] = xj[:, 0:NODES]
            substep_some(work, reactions_of(species_ref, rate_ref, GAIN), 32, 48, False)
            for cut in range(2):
                out_ref[STRIDE - 1, :, :, half(cut)] = (
                    own_result(work, cut) + base_ref[:, :, half(cut)]
                )

        w[0:NODES, :] = fine_ref[...]
        xj[:, 0:NODES] = begin[...]
        reactions = reactions_of(species_ref, rate_ref, 1.0)

        def fine(number, carry):
            substep(work, reactions, keep(work))

            @pl.when(number == 1)
            def _():
                for cut in range(2):
                    out_ref[0, :, :, half(cut)] = own_result(work, cut)

            return carry

        lax.fori_loop(0, 3, fine, 0)
        substep_some(work, reactions, 16, 64, True)
        for cut in range(2):
            out_ref[1, :, :, half(cut)] = own_result(work, cut)
        substep_some(work, reactions, 16, 48, True)
        substep_some(work, reactions, 32, 48, False)
        for cut in range(2):
            out_ref[2, :, :, half(cut)] = own_result(work, cut)


class Work:
    def __init__(self, refs, table, face, speed):
        self.xj, self.s, self.w = refs[:3]
        self.t, self.plus, self.minus, self.square = (refs[i : i + 2] for i in (3, 5, 7, 9))
        self.table, self.face, self.speed = table, face, speed


VMEM_SPEC = pl.BlockSpec(memory_space=pltpu.VMEM)
SMEM_SPEC = pl.BlockSpec(memory_space=pltpu.SMEM)


def work_buffers():
    return [
        pltpu.VMEM((ROWS, NODES + FACES), BF),
        pltpu.VMEM((ROWS, FACES), BF),
        pltpu.VMEM((NODES + FACES, NODES), BF),
    ] + [pltpu.VMEM((VARS, ELEMS, HALF), F32)] * 8


def body(
    coarse_guess,
    initial_state,
    fine_volume,
    coarse_volume,
    lift_matrix,
    wave_speed,
    reaction_rate,
    species_map,
    neighbour_element,
    neighbour_rank,
):
    group = lax.axis_index("tm")
    groups = lax.axis_size("tm")
    start = jnp.where((group == 0) | (group == groups - 1), initial_state, coarse_guess[0])
    start = jnp.transpose(start, (1, 0, 2)).reshape(VARS * BLOCK, NODES).astype(BF)
    code = ((neighbour_rank + 1) * BLOCK + neighbour_element).astype(BF)
    code = jnp.pad(code, ((0, 8), (0, NODES - 6)))
    payload = jnp.concatenate([start, code], axis=0)
    def sent(array, place):
        pairs = []
        for source in range(groups):
            for block in range(BLOCKS):
                target, there = place(source, block)
                pairs.append((source * BLOCKS + block, target % groups * BLOCKS + there % BLOCKS))
        return lax.ppermute(array, ("tm", "space"), pairs)

    near = sent(payload, lambda i, s: (i + 1, s))
    far = sent(payload, lambda i, s: (i + 1, s ^ 1))
    here = jnp.concatenate([near, far], axis=0)
    parts = [
        sent(here, lambda i, s: (i, s + 4)),
        sent(here, lambda i, s: (i, s + 2)),
        here,
        sent(here, lambda i, s: (i, s - 2)),
    ]
    face_table = jnp.asarray(swapped_face_table()).astype(BF)
    group_array = jnp.stack([group, lax.axis_index("space") % 2]).astype(jnp.int32)
    params = pltpu.CompilerParams(vmem_limit_bytes=56 * 1024 * 1024)
    send, base, second, table = pl.pallas_call(
        relax_kernel,
        out_shape=(
            jax.ShapeDtypeStruct((ROWS, NODES), BF),
            jax.ShapeDtypeStruct((VARS, BLOCK, NODES), F32),
            jax.ShapeDtypeStruct((ROWS, NODES), BF),
            jax.ShapeDtypeStruct((3, ELEMS, 128), BF),
        ),
        in_specs=[SMEM_SPEC] * 4 + [VMEM_SPEC] * 8,
        out_specs=(VMEM_SPEC,) * 4,
        scratch_shapes=work_buffers() + [pltpu.VMEM((VARS, ELEMS, HALF), F32)] * 2,
        compiler_params=params,
    )(
        group_array, species_map, reaction_rate, wave_speed,
        *parts, face_table, fine_volume, coarse_volume, lift_matrix,
    )
    terms = lax.all_gather(send, "tm", axis=0, tiled=False)
    full = lambda *shape: pl.BlockSpec(shape, lambda k: (0,) * len(shape))
    out = pl.pallas_call(
        chain_kernel,
        grid=(13,),
        out_shape=jax.ShapeDtypeStruct((STRIDE, VARS, BLOCK, NODES), F32),
        in_specs=[SMEM_SPEC] * 4
        + [
            pl.BlockSpec((1, ROWS, NODES), lambda k: (1, 0, 0)),
            pl.BlockSpec((1, ROWS, NODES), lambda k: (k + 2, 0, 0)),
            full(ROWS, NODES),
            full(VARS, BLOCK, NODES),
            full(3, ELEMS, 128),
            full(NODES, 256),
            full(NODES, NODES),
            full(NODES, NODES),
            full(FACES, NODES),
        ],
        out_specs=full(STRIDE, VARS, BLOCK, NODES),
        scratch_shapes=work_buffers() + [pltpu.VMEM((ROWS, NODES), BF)],
        compiler_params=params,
    )(
        group_array, species_map, reaction_rate, wave_speed,
        terms, terms, second, base, table, face_table, fine_volume, coarse_volume, lift_matrix,
    )
    return jnp.transpose(out, (0, 2, 1, 3))


def solution(mesh):
    placed = (
        P("tm", "space", None, None),
        P("space", None, None),
        P(),
        P(),
        P(),
        P(),
        P(),
        P(),
        P("space", None),
        P("space", None),
    )
    return jax.shard_map(
        body, mesh=mesh, in_specs=placed, out_specs=P("tm", "space", None, None), check_vma=False
    )
```

```python
import jax
import jax.numpy as jnp
import numpy as np
from jax import lax
from jax.experimental import pallas as pl
from jax.experimental.pallas import tpu as pltpu
from jax.sharding import PartitionSpec as P

SIDE = 8
NODES = 512
FACES = 384
VARS = 12
REACTIONS = 24
BLOCK = 8
BLOCKS = 8
ELEMS = 64
ROWS = VARS * ELEMS
HALF = NODES // 2
PAYLOAD = 112
THIRD = ROWS // 3
OWN = 4
STRIDE = 4
GAIN = 4.0
BF = jnp.bfloat16
F32 = jnp.float32


def swapped_face_table():
    inner = np.arange(64)
    first, second = inner // 8, inner % 8
    nodes = [
        first * 64 + second,
        first * 64 + 56 + second,
        first * 64 + second * 8,
        first * 64 + second * 8 + 7,
    ]
    table = np.zeros((NODES, 256), np.float32)
    for place, face in enumerate((1, 0, 3, 2)):
        table[nodes[face], place * 64 + inner] = 1.0
    return table


def gather_tables(code, table_ref):
    row = lax.broadcasted_iota(jnp.int32, (ELEMS, ELEMS), 0)
    column = lax.broadcasted_iota(jnp.int32, (ELEMS, ELEMS), 1)
    home = row - jnp.bitwise_and(row, 7)
    for pair in range(3):
        parts = []
        for face in (2 * pair, 2 * pair + 1):
            source = jnp.bitwise_and(home + code[:, face : face + 1] + 56, 63)
            parts.append(jnp.where(source == column, 1.0, 0.0))
        table_ref[pair] = jnp.concatenate(parts, axis=1).astype(BF)


def exchange(xj_ref, s_ref, table_ref, face_ref, speed_ref, low, high):
    lane = lax.broadcasted_iota(jnp.int32, (ELEMS, 128), 1)
    left = lane < 64
    zero = jnp.zeros((ELEMS, 128), BF)
    s_ref[:, 128:384] = jnp.dot(
        xj_ref[:, 0:NODES], face_ref[...], preferred_element_type=F32
    ).astype(BF)
    lo = xj_ref[:, 0:128]
    hi = xj_ref[:, NODES - 128 : NODES]
    s_ref[:, 0:128] = jnp.concatenate([hi[:, 64:128], lo[:, 0:64]], axis=1)
    for v in range(0, VARS, 2):
        for pair in range(3):
            lanes = slice(pair * 128, (pair + 1) * 128)
            stacks = []
            for half in range(2):
                swapped = s_ref[(v + half) * ELEMS : (v + half + 1) * ELEMS, lanes]
                stacks.append(
                    jnp.concatenate(
                        [jnp.where(left, swapped, zero), jnp.where(left, zero, swapped)], axis=0
                    )
                )
            across = jnp.dot(
                table_ref[pair, low:high], jnp.concatenate(stacks, axis=1), preferred_element_type=F32
            )
            for half in range(2):
                rows = slice((v + half) * ELEMS + low, (v + half) * ELEMS + high)
                swapped = s_ref[rows, lanes]
                own = jnp.concatenate([swapped[:, 64:128], swapped[:, 0:64]], axis=1).astype(F32)
                xj_ref[rows, NODES + pair * 128 : NODES + (pair + 1) * 128] = (
                    (across[:, half * 128 : (half + 1) * 128] - own) * speed_ref[v + half]
                ).astype(BF)


def move(xj_ref, w_ref, t_ref, cut, row, rows):
    moved = jnp.dot(
        xj_ref[row : row + rows, :],
        w_ref[:, cut * HALF : (cut + 1) * HALF],
        preferred_element_type=F32,
    )
    t_ref[row // ELEMS : (row + rows) // ELEMS] = moved.reshape(rows // ELEMS, ELEMS, HALF)


def move_some(xj_ref, w_ref, t_ref, cut, low, high):
    rows = jnp.concatenate([xj_ref[v * ELEMS + low : v * ELEMS + high, :] for v in range(VARS)], axis=0)
    moved = jnp.dot(
        rows, w_ref[:, cut * HALF : (cut + 1) * HALF], preferred_element_type=F32
    )
    t_ref[:, low:high, :] = moved.reshape(VARS, high - low, HALF)


def prepare(work, cut, low, high):
    rows = slice(low, high)
    t = work.t[cut][:, rows, :]
    work.plus[cut][:, rows, :] = t
    work.square[cut][:, rows, :] = 0.5 + t * t
    work.minus[cut][:, rows, :] = jnp.zeros_like(t)


def react(work, cut, reaction, low, high):
    first, second, made, scale = reaction
    rows = slice(low, high)
    t, square = work.t[cut], work.square[cut]
    rate = scale * (t[first, rows] * t[second, rows]) / (square[first, rows] + square[second, rows])
    work.plus[cut][made, rows] += rate
    work.minus[cut][first, rows] += rate


def result(work, cut, low=0, high=ELEMS):
    return work.plus[cut][:, low:high, :] - work.minus[cut][:, low:high, :]


def own_result(work, cut):
    return result(work, cut, OWN * BLOCK, (OWN + 1) * BLOCK)


def substep(work, reactions, finish):
    exchange(work.xj, work.s, work.table, work.face, work.speed, 0, ELEMS)
    move(work.xj, work.w, work.t[0], 0, 0, ROWS)
    prepare(work, 0, 0, ELEMS)
    for number, reaction in enumerate(reactions):
        react(work, 0, reaction, 0, ELEMS)
        if number % 4 == 1:
            move(work.xj, work.w, work.t[1], 1, number // 4 * 128, 128)
    finish(0)
    prepare(work, 1, 0, ELEMS)
    for reaction in reactions:
        react(work, 1, reaction, 0, ELEMS)
    finish(1)


def substep_some(work, reactions, low, high, store):
    exchange(work.xj, work.s, work.table, work.face, work.speed, low, high)
    for cut in range(2):
        move_some(work.xj, work.w, work.t[cut], cut, low, high)
    for cut in range(2):
        prepare(work, cut, low, high)
        for reaction in reactions:
            react(work, cut, reaction, low, high)
        if store:
            value = result(work, cut, low, high).astype(BF)
            for v in range(VARS):
                work.xj[v * ELEMS + low : v * ELEMS + high, half(cut)] = value[v]


def reactions_of(species_ref, rate_ref, gain):
    return [
        (species_ref[r, 0], species_ref[r, 1], species_ref[r, 2], gain * rate_ref[r])
        for r in range(REACTIONS)
    ]


def half(cut):
    return slice(cut * HALF, (cut + 1) * HALF)


def keep(work):
    def finish(cut):
        work.xj[:, half(cut)] = result(work, cut).astype(BF).reshape(ROWS, HALF)

    return finish


def relax_kernel(group_ref, species_ref, rate_ref, speed_ref, *refs):
    pairs = refs[:4]
    face_ref, fine_ref, coarse_ref, lift_ref = refs[4:8]
    send_ref, base_ref, second_ref, table_ref = refs[8:12]
    work = Work(refs[12:-2], table_ref, face_ref, speed_ref)
    stepped = refs[-2:]
    xj, w = work.xj, work.w
    group = group_ref[0]
    even = group_ref[1] == 0
    near = [pair[0:PAYLOAD].astype(F32) for pair in pairs]
    far = [pair[PAYLOAD:].astype(F32) for pair in pairs]
    values = []
    for k in range(4):
        values += [near[k], jnp.where(even, far[k], far[(k + 1) % 4])]
    for v in range(VARS):
        rows = jnp.concatenate([p[v * BLOCK : (v + 1) * BLOCK] for p in values], axis=0)
        xj[v * ELEMS : (v + 1) * ELEMS, 0:NODES] = rows.astype(BF)
    codes = jnp.concatenate([p[VARS * BLOCK : (VARS + 1) * BLOCK, 0:128] for p in values], axis=0)
    gather_tables(codes.astype(jnp.int32), table_ref)
    w[0:NODES, :] = fine_ref[...]
    w[NODES:, :] = lift_ref[...]
    second_ref[...] = xj[:, 0:NODES]
    reactions = reactions_of(species_ref, rate_ref, 1.0)

    def fine(index, carry):
        substep(work, reactions, keep(work))
        return carry

    lax.fori_loop(0, 8, fine, 0)

    @pl.when(group == 0)
    def _():
        xj[:, 0:NODES] = second_ref[...]

    second_ref[...] = xj[:, 0:NODES]
    w[0:NODES, :] = coarse_ref[...]

    def hold(cut):
        stepped[cut][...] = result(work, cut)

    substep(work, reactions_of(species_ref, rate_ref, GAIN), hold)
    w[0:NODES, :] = fine_ref[...]
    lax.fori_loop(0, 8, fine, 0)
    own = slice(OWN * BLOCK, (OWN + 1) * BLOCK)
    for cut in range(2):
        last = result(work, cut)
        term = last - stepped[cut][...]
        send_ref[:, half(cut)] = jnp.where(group == 1, last, term).astype(BF).reshape(ROWS, HALF)
        base_ref[:, :, half(cut)] = jnp.where(group <= 1, last[:, own], term[:, own])


def chain_kernel(group_ref, species_ref, rate_ref, speed_ref, *refs):
    terms = refs[:20]
    second_ref, base_ref, table_ref, face_ref, fine_ref, coarse_ref, lift_ref, out_ref = refs[20:28]
    work = Work(refs[28:-3], table_ref, face_ref, speed_ref)
    begin, term_buffer, arrived = refs[-3:]
    xj, w = work.xj, work.w
    group = group_ref[0]

    def fetch(item, slot):
        other_z = jnp.bitwise_xor(item, group) & 8
        distance = ((item >> 1) - (group >> 1)) & 3
        place = other_z + 2 * distance + (jnp.bitwise_xor(item, group) & 1)

        def copy(source, rows):
            pltpu.make_async_copy(source, term_buffer.at[slot, rows], arrived.at[slot]).start()

        whole = [n for n in range(16) if n not in (12, 13)]
        for number, n in enumerate(whole):

            @pl.when(place == n)
            def _(number=number):
                copy(terms[number], pl.ds(0, ROWS))

        for n in (12, 13):

            @pl.when(place == n)
            def _(n=n):
                for third in range(3):
                    copy(terms[14 + third + 3 * (n - 12)], pl.ds(third * THIRD, THIRD))

    def await_term(slot):
        pltpu.make_async_copy(terms[0], term_buffer.at[slot], arrived.at[slot]).wait()

    fetch(1, 1)
    w[0:NODES, :] = coarse_ref[...]
    w[NODES:, :] = lift_ref[...]
    begin[...] = second_ref[...]
    out_ref[STRIDE - 1] = base_ref[...]
    await_term(1)
    xj[:, 0:NODES] = term_buffer[1]
    fetch(2, 0)
    coarse_reactions = reactions_of(species_ref, rate_ref, GAIN)

    def chain(index, carry):
        slot = index & 1
        await_term(slot)

        @pl.when(index < 14)
        def _():
            fetch(index + 1, 1 - slot)

        @pl.when(index == group)
        def _():
            begin[...] = xj[:, 0:NODES]

        def chained(cut):
            term = term_buffer[slot, :, half(cut)].astype(F32)
            xj[:, half(cut)] = (result(work, cut).reshape(ROWS, HALF) + term).astype(BF)

        substep(work, coarse_reactions, chained)

        @pl.when(index == group)
        def _():
            for cut in range(2):
                out_ref[STRIDE - 1, :, :, half(cut)] = (
                    own_result(work, cut) + base_ref[:, :, half(cut)]
                )

        return carry

    lax.fori_loop(2, 15, chain, 0)

    @pl.when(group == 15)
    def _():
        begin[...] = xj[:, 0:NODES]
        substep_some(work, coarse_reactions, 32, 48, False)
        for cut in range(2):
            out_ref[STRIDE - 1, :, :, half(cut)] = (
                own_result(work, cut) + base_ref[:, :, half(cut)]
            )

    w[0:NODES, :] = fine_ref[...]
    xj[:, 0:NODES] = begin[...]
    reactions = reactions_of(species_ref, rate_ref, 1.0)

    def fine(number, carry):
        substep(work, reactions, keep(work))

        @pl.when(number == 1)
        def _():
            for cut in range(2):
                out_ref[0, :, :, half(cut)] = own_result(work, cut)

        return carry

    lax.fori_loop(0, 3, fine, 0)
    substep_some(work, reactions, 16, 64, True)
    for cut in range(2):
        out_ref[1, :, :, half(cut)] = own_result(work, cut)
    substep_some(work, reactions, 16, 48, True)
    substep_some(work, reactions, 32, 48, False)
    for cut in range(2):
        out_ref[2, :, :, half(cut)] = own_result(work, cut)


class Work:
    def __init__(self, refs, table, face, speed):
        self.xj, self.s, self.w = refs[:3]
        self.t, self.plus, self.minus, self.square = (refs[i : i + 2] for i in (3, 5, 7, 9))
        self.table, self.face, self.speed = table, face, speed


VMEM_SPEC = pl.BlockSpec(memory_space=pltpu.VMEM)
SMEM_SPEC = pl.BlockSpec(memory_space=pltpu.SMEM)


def work_buffers():
    return [
        pltpu.VMEM((ROWS, NODES + FACES), BF),
        pltpu.VMEM((ROWS, FACES), BF),
        pltpu.VMEM((NODES + FACES, NODES), BF),
    ] + [pltpu.VMEM((VARS, ELEMS, HALF), F32)] * 8


def body(
    coarse_guess,
    initial_state,
    fine_volume,
    coarse_volume,
    lift_matrix,
    wave_speed,
    reaction_rate,
    species_map,
    neighbour_element,
    neighbour_rank,
):
    group = lax.axis_index("tm")
    groups = lax.axis_size("tm")
    start = jnp.where((group == 0) | (group == groups - 1), initial_state, coarse_guess[0])
    start = jnp.transpose(start, (1, 0, 2)).reshape(VARS * BLOCK, NODES).astype(BF)
    code = ((neighbour_rank + 1) * BLOCK + neighbour_element).astype(BF)
    code = jnp.pad(code, ((0, 8), (0, NODES - 6)))
    payload = jnp.concatenate([start, code], axis=0)
    def sent(array, place):
        pairs = []
        for source in range(groups):
            for block in range(BLOCKS):
                target, there = place(source, block)
                pairs.append((source * BLOCKS + block, target % groups * BLOCKS + there % BLOCKS))
        return lax.ppermute(array, ("tm", "space"), pairs)

    near = sent(payload, lambda i, s: (i + 1, s))
    far = sent(payload, lambda i, s: (i + 1, s ^ 1))
    here = jnp.concatenate([near, far], axis=0)
    parts = [
        sent(here, lambda i, s: (i, s + 4)),
        sent(here, lambda i, s: (i, s + 2)),
        here,
        sent(here, lambda i, s: (i, s - 2)),
    ]
    face_table = jnp.asarray(swapped_face_table()).astype(BF)
    group_array = jnp.stack([group, lax.axis_index("space") % 2]).astype(jnp.int32)
    params = pltpu.CompilerParams(vmem_limit_bytes=56 * 1024 * 1024)
    send, base, second, table = pl.pallas_call(
        relax_kernel,
        out_shape=(
            jax.ShapeDtypeStruct((ROWS, NODES), BF),
            jax.ShapeDtypeStruct((VARS, BLOCK, NODES), F32),
            jax.ShapeDtypeStruct((ROWS, NODES), BF),
            jax.ShapeDtypeStruct((3, ELEMS, 128), BF),
        ),
        in_specs=[SMEM_SPEC] * 4 + [VMEM_SPEC] * 8,
        out_specs=(VMEM_SPEC,) * 4,
        scratch_shapes=work_buffers() + [pltpu.VMEM((VARS, ELEMS, HALF), F32)] * 2,
        compiler_params=params,
    )(
        group_array, species_map, reaction_rate, wave_speed,
        *parts, face_table, fine_volume, coarse_volume, lift_matrix,
    )

    def over(array, other_z, along_x, other_core):
        def place(i, s):
            z, x, core = i // 8, i // 2 % 4, i % 2
            return (z ^ other_z) * 8 + (x + along_x) % 4 * 2 + (core ^ other_core), s

        return sent(array, place)

    low, middle, high = (slice(k * THIRD, (k + 1) * THIRD) for k in range(3))
    below, above, across = over(send, 0, 1, 0), over(send, 0, -1, 0), over(send, 1, 0, 0)
    send_pair = over(send, 0, 0, 1)
    far_x, across_above, across_below = over(below, 0, 1, 0), over(across, 0, -1, 0), over(below, 1, 0, 0)
    below_pair, above_pair, across_pair = (over(item, 0, 0, 1) for item in (below, above, across))
    last = [
        over(across_above[low], 0, -1, 0),
        over(across_below[middle], 0, 1, 0),
        over(far_x[high], 1, 0, 0),
    ]
    far_pair, across_above_pair, across_below_pair = (
        over(item, 0, 0, 1) for item in (far_x, across_above, across_below)
    )
    last_pair = [over(item, 0, 0, 1) for item in last]
    terms = [
        send, send_pair, above, above_pair, far_x, far_pair, below, below_pair,
        across, across_pair, across_above, across_above_pair, across_below, across_below_pair,
        *last, *last_pair,
    ]
    out = pl.pallas_call(
        chain_kernel,
        out_shape=jax.ShapeDtypeStruct((STRIDE, VARS, BLOCK, NODES), F32),
        in_specs=[SMEM_SPEC] * 4 + [pl.BlockSpec(memory_space=pl.ANY)] * 20 + [VMEM_SPEC] * 7,
        out_specs=VMEM_SPEC,
        scratch_shapes=work_buffers()
        + [
            pltpu.VMEM((ROWS, NODES), BF),
            pltpu.VMEM((2, ROWS, NODES), BF),
            pltpu.SemaphoreType.DMA((2,)),
        ],
        compiler_params=params,
    )(
        group_array, species_map, reaction_rate, wave_speed,
        *terms, second, base, table, face_table, fine_volume, coarse_volume, lift_matrix,
    )
    return jnp.transpose(out, (0, 2, 1, 3))


def solution(mesh):
    placed = (
        P("tm", "space", None, None),
        P("space", None, None),
        P(),
        P(),
        P(),
        P(),
        P(),
        P(),
        P("space", None),
        P("space", None),
    )
    return jax.shard_map(
        body, mesh=mesh, in_specs=placed, out_specs=P("tm", "space", None, None), check_vma=False
    )
```

```python
import jax
import jax.numpy as jnp
import numpy as np
from jax import lax
from jax.experimental import pallas as pl
from jax.experimental.pallas import tpu as pltpu
from jax.sharding import PartitionSpec as P

SIDE = 8
NODES = 512
FACES = 384
VARS = 12
REACTIONS = 24
BLOCK = 8
BLOCKS = 8
ELEMS = 64
ROWS = VARS * ELEMS
HALF = NODES // 2
PAYLOAD = 112
THIRD = ROWS // 3
OWN = 4
STRIDE = 4
GAIN = 4.0
BF = jnp.bfloat16
F32 = jnp.float32


def swapped_face_table():
    inner = np.arange(64)
    first, second = inner // 8, inner % 8
    nodes = [
        first * 64 + second,
        first * 64 + 56 + second,
        first * 64 + second * 8,
        first * 64 + second * 8 + 7,
    ]
    table = np.zeros((NODES, 256), np.float32)
    for place, face in enumerate((1, 0, 3, 2)):
        table[nodes[face], place * 64 + inner] = 1.0
    return table


def gather_tables(code, table_ref):
    row = lax.broadcasted_iota(jnp.int32, (ELEMS, ELEMS), 0)
    column = lax.broadcasted_iota(jnp.int32, (ELEMS, ELEMS), 1)
    home = row - jnp.bitwise_and(row, 7)
    for pair in range(3):
        parts = []
        for face in (2 * pair, 2 * pair + 1):
            source = jnp.bitwise_and(home + code[:, face : face + 1] + 56, 63)
            parts.append(jnp.where(source == column, 1.0, 0.0))
        table_ref[pair] = jnp.concatenate(parts, axis=1).astype(BF)


def exchange(xj_ref, s_ref, table_ref, face_ref, speed_ref, low, high):
    lane = lax.broadcasted_iota(jnp.int32, (ELEMS, 128), 1)
    left = lane < 64
    zero = jnp.zeros((ELEMS, 128), BF)
    s_ref[:, 128:384] = jnp.dot(
        xj_ref[:, 0:NODES], face_ref[...], preferred_element_type=F32
    ).astype(BF)
    lo = xj_ref[:, 0:128]
    hi = xj_ref[:, NODES - 128 : NODES]
    s_ref[:, 0:128] = jnp.concatenate([hi[:, 64:128], lo[:, 0:64]], axis=1)
    for v in range(0, VARS, 2):
        for pair in range(3):
            lanes = slice(pair * 128, (pair + 1) * 128)
            stacks = []
            for half in range(2):
                swapped = s_ref[(v + half) * ELEMS : (v + half + 1) * ELEMS, lanes]
                stacks.append(
                    jnp.concatenate(
                        [jnp.where(left, swapped, zero), jnp.where(left, zero, swapped)], axis=0
                    )
                )
            across = jnp.dot(
                table_ref[pair, low:high], jnp.concatenate(stacks, axis=1), preferred_element_type=F32
            )
            for half in range(2):
                rows = slice((v + half) * ELEMS + low, (v + half) * ELEMS + high)
                swapped = s_ref[rows, lanes]
                own = jnp.concatenate([swapped[:, 64:128], swapped[:, 0:64]], axis=1).astype(F32)
                xj_ref[rows, NODES + pair * 128 : NODES + (pair + 1) * 128] = (
                    (across[:, half * 128 : (half + 1) * 128] - own) * speed_ref[v + half]
                ).astype(BF)


def move(xj_ref, w_ref, t_ref, cut, row, rows):
    moved = jnp.dot(
        xj_ref[row : row + rows, :],
        w_ref[:, cut * HALF : (cut + 1) * HALF],
        preferred_element_type=F32,
    )
    t_ref[row // ELEMS : (row + rows) // ELEMS] = moved.reshape(rows // ELEMS, ELEMS, HALF)


def move_some(xj_ref, w_ref, t_ref, cut, low, high):
    rows = jnp.concatenate([xj_ref[v * ELEMS + low : v * ELEMS + high, :] for v in range(VARS)], axis=0)
    moved = jnp.dot(
        rows, w_ref[:, cut * HALF : (cut + 1) * HALF], preferred_element_type=F32
    )
    t_ref[:, low:high, :] = moved.reshape(VARS, high - low, HALF)


def prepare(work, cut, low, high):
    rows = slice(low, high)
    t = work.t[cut][:, rows, :]
    work.plus[cut][:, rows, :] = t
    work.square[cut][:, rows, :] = 0.5 + t * t
    work.minus[cut][:, rows, :] = jnp.zeros_like(t)


def react(work, cut, reaction, low, high):
    first, second, made, scale = reaction
    rows = slice(low, high)
    t, square = work.t[cut], work.square[cut]
    rate = scale * (t[first, rows] * t[second, rows]) / (square[first, rows] + square[second, rows])
    work.plus[cut][made, rows] += rate
    work.minus[cut][first, rows] += rate


def result(work, cut, low=0, high=ELEMS):
    return work.plus[cut][:, low:high, :] - work.minus[cut][:, low:high, :]


def own_result(work, cut):
    return result(work, cut, OWN * BLOCK, (OWN + 1) * BLOCK)


def substep(work, reactions, finish):
    exchange(work.xj, work.s, work.table, work.face, work.speed, 0, ELEMS)
    move(work.xj, work.w, work.t[0], 0, 0, ROWS)
    prepare(work, 0, 0, ELEMS)
    for number, reaction in enumerate(reactions):
        react(work, 0, reaction, 0, ELEMS)
        if number % 4 == 1:
            move(work.xj, work.w, work.t[1], 1, number // 4 * 128, 128)
    finish(0)
    prepare(work, 1, 0, ELEMS)
    for reaction in reactions:
        react(work, 1, reaction, 0, ELEMS)
    finish(1)


def substep_some(work, reactions, low, high, store):
    exchange(work.xj, work.s, work.table, work.face, work.speed, low, high)
    for cut in range(2):
        move_some(work.xj, work.w, work.t[cut], cut, low, high)
    for cut in range(2):
        prepare(work, cut, low, high)
        for reaction in reactions:
            react(work, cut, reaction, low, high)
        if store:
            value = result(work, cut, low, high).astype(BF)
            for v in range(VARS):
                work.xj[v * ELEMS + low : v * ELEMS + high, half(cut)] = value[v]


def reactions_of(species_ref, rate_ref, gain):
    return [
        (species_ref[r, 0], species_ref[r, 1], species_ref[r, 2], gain * rate_ref[r])
        for r in range(REACTIONS)
    ]


def half(cut):
    return slice(cut * HALF, (cut + 1) * HALF)


def keep(work):
    def finish(cut):
        work.xj[:, half(cut)] = result(work, cut).astype(BF).reshape(ROWS, HALF)

    return finish


def relax_kernel(group_ref, species_ref, rate_ref, speed_ref, *refs):
    pairs = refs[:4]
    face_ref, fine_ref, coarse_ref, lift_ref = refs[4:8]
    send_ref, base_ref, second_ref, table_ref = refs[8:12]
    work = Work(refs[12:-2], table_ref, face_ref, speed_ref)
    stepped = refs[-2:]
    xj, w = work.xj, work.w
    group = group_ref[0]
    even = group_ref[1] == 0
    near = [pair[0:PAYLOAD].astype(F32) for pair in pairs]
    far = [pair[PAYLOAD:].astype(F32) for pair in pairs]
    values = []
    for k in range(4):
        values += [near[k], jnp.where(even, far[k], far[(k + 1) % 4])]
    for v in range(VARS):
        rows = jnp.concatenate([p[v * BLOCK : (v + 1) * BLOCK] for p in values], axis=0)
        xj[v * ELEMS : (v + 1) * ELEMS, 0:NODES] = rows.astype(BF)
    codes = jnp.concatenate([p[VARS * BLOCK : (VARS + 1) * BLOCK, 0:128] for p in values], axis=0)
    gather_tables(codes.astype(jnp.int32), table_ref)
    w[0:NODES, :] = fine_ref[...]
    w[NODES:, :] = lift_ref[...]
    second_ref[...] = xj[:, 0:NODES]
    reactions = reactions_of(species_ref, rate_ref, 1.0)

    def fine(index, carry):
        substep(work, reactions, keep(work))
        return carry

    lax.fori_loop(0, 8, fine, 0)

    @pl.when(group == 0)
    def _():
        xj[:, 0:NODES] = second_ref[...]

    second_ref[...] = xj[:, 0:NODES]
    w[0:NODES, :] = coarse_ref[...]

    def hold(cut):
        stepped[cut][...] = result(work, cut)

    substep(work, reactions_of(species_ref, rate_ref, GAIN), hold)
    w[0:NODES, :] = fine_ref[...]
    lax.fori_loop(0, 8, fine, 0)
    own = slice(OWN * BLOCK, (OWN + 1) * BLOCK)
    for cut in range(2):
        last = result(work, cut)
        term = last - stepped[cut][...]
        send_ref[:, half(cut)] = jnp.where(group == 1, last, term).astype(BF).reshape(ROWS, HALF)
        base_ref[:, :, half(cut)] = jnp.where(group <= 1, last[:, own], term[:, own])


def chain_kernel(group_ref, species_ref, rate_ref, speed_ref, *refs):
    terms = refs[:20]
    second_ref, base_ref, table_ref, face_ref, fine_ref, coarse_ref, lift_ref, out_ref = refs[20:28]
    work = Work(refs[28:-3], table_ref, face_ref, speed_ref)
    begin, term_buffer, arrived = refs[-3:]
    xj, w = work.xj, work.w
    group = group_ref[0]

    def fetch(item, slot):
        other_z = jnp.bitwise_xor(item, group) & 8
        distance = ((item >> 1) - (group >> 1)) & 3
        place = other_z + 2 * distance + (jnp.bitwise_xor(item, group) & 1)

        def copy(source, rows):
            pltpu.make_async_copy(source, term_buffer.at[slot, rows], arrived.at[slot]).start()

        whole = [n for n in range(16) if n not in (12, 13)]
        for number, n in enumerate(whole):

            @pl.when(place == n)
            def _(number=number):
                copy(terms[number], pl.ds(0, ROWS))

        for n in (12, 13):

            @pl.when(place == n)
            def _(n=n):
                for third in range(3):
                    copy(terms[14 + third + 3 * (n - 12)], pl.ds(third * THIRD, THIRD))

    def await_term(slot):
        pltpu.make_async_copy(terms[0], term_buffer.at[slot], arrived.at[slot]).wait()

    fetch(1, 1)
    w[0:NODES, :] = coarse_ref[...]
    w[NODES:, :] = lift_ref[...]
    begin[...] = second_ref[...]
    out_ref[STRIDE - 1] = base_ref[...]
    await_term(1)
    xj[:, 0:NODES] = term_buffer[1]
    fetch(2, 0)
    coarse_reactions = reactions_of(species_ref, rate_ref, GAIN)

    def chain(index, carry):
        slot = index & 1
        await_term(slot)

        @pl.when(index < 14)
        def _():
            fetch(index + 1, 1 - slot)

        @pl.when(index == group)
        def _():
            begin[...] = xj[:, 0:NODES]

        def chained(cut):
            term = term_buffer[slot, :, half(cut)].astype(F32)
            xj[:, half(cut)] = (result(work, cut).reshape(ROWS, HALF) + term).astype(BF)

        substep(work, coarse_reactions, chained)

        @pl.when(index == group)
        def _():
            for cut in range(2):
                out_ref[STRIDE - 1, :, :, half(cut)] = (
                    own_result(work, cut) + base_ref[:, :, half(cut)]
                )

        return carry

    lax.fori_loop(2, 15, chain, 0)

    @pl.when(group == 15)
    def _():
        begin[...] = xj[:, 0:NODES]
        substep_some(work, coarse_reactions, 32, 48, False)
        for cut in range(2):
            out_ref[STRIDE - 1, :, :, half(cut)] = (
                own_result(work, cut) + base_ref[:, :, half(cut)]
            )

    w[0:NODES, :] = fine_ref[...]
    xj[:, 0:NODES] = begin[...]
    reactions = reactions_of(species_ref, rate_ref, 1.0)

    def fine(number, carry):
        substep(work, reactions, keep(work))

        @pl.when(number == 1)
        def _():
            for cut in range(2):
                out_ref[0, :, :, half(cut)] = own_result(work, cut)

        return carry

    lax.fori_loop(0, 3, fine, 0)
    substep_some(work, reactions, 16, 64, True)
    for cut in range(2):
        out_ref[1, :, :, half(cut)] = own_result(work, cut)
    substep_some(work, reactions, 16, 48, True)
    substep_some(work, reactions, 32, 48, False)
    for cut in range(2):
        out_ref[2, :, :, half(cut)] = own_result(work, cut)


class Work:
    def __init__(self, refs, table, face, speed):
        self.xj, self.s, self.w = refs[:3]
        self.t, self.plus, self.minus, self.square = (refs[i : i + 2] for i in (3, 5, 7, 9))
        self.table, self.face, self.speed = table, face, speed


VMEM_SPEC = pl.BlockSpec(memory_space=pltpu.VMEM)
SMEM_SPEC = pl.BlockSpec(memory_space=pltpu.SMEM)


def work_buffers():
    return [
        pltpu.VMEM((ROWS, NODES + FACES), BF),
        pltpu.VMEM((ROWS, FACES), BF),
        pltpu.VMEM((NODES + FACES, NODES), BF),
    ] + [pltpu.VMEM((VARS, ELEMS, HALF), F32)] * 8


def body(
    coarse_guess,
    initial_state,
    fine_volume,
    coarse_volume,
    lift_matrix,
    wave_speed,
    reaction_rate,
    species_map,
    neighbour_element,
    neighbour_rank,
):
    group = lax.axis_index("tm")
    groups = lax.axis_size("tm")
    start = jnp.where((group == 0) | (group == groups - 1), initial_state, coarse_guess[0])
    start = jnp.transpose(start, (1, 0, 2)).reshape(VARS * BLOCK, NODES).astype(BF)
    code = ((neighbour_rank + 1) * BLOCK + neighbour_element).astype(BF)
    code = jnp.pad(code, ((0, 8), (0, NODES - 6)))
    payload = jnp.concatenate([start, code], axis=0)
    def sent(array, place):
        pairs = []
        for source in range(groups):
            for block in range(BLOCKS):
                target, there = place(source, block)
                pairs.append((source * BLOCKS + block, target % groups * BLOCKS + there % BLOCKS))
        return lax.ppermute(array, ("tm", "space"), pairs)

    near = sent(payload, lambda i, s: (i + 1, s))
    far = sent(payload, lambda i, s: (i + 1, s ^ 1))
    here = jnp.concatenate([near, far], axis=0)
    parts = [
        sent(here, lambda i, s: (i, s + 4)),
        sent(here, lambda i, s: (i, s + 2)),
        here,
        sent(here, lambda i, s: (i, s - 2)),
    ]
    face_table = jnp.asarray(swapped_face_table()).astype(BF)
    group_array = jnp.stack([group, lax.axis_index("space") % 2]).astype(jnp.int32)
    params = pltpu.CompilerParams(vmem_limit_bytes=56 * 1024 * 1024)
    send, base, second, table = pl.pallas_call(
        relax_kernel,
        out_shape=(
            jax.ShapeDtypeStruct((ROWS, NODES), BF),
            jax.ShapeDtypeStruct((VARS, BLOCK, NODES), F32),
            jax.ShapeDtypeStruct((ROWS, NODES), BF),
            jax.ShapeDtypeStruct((3, ELEMS, 128), BF),
        ),
        in_specs=[SMEM_SPEC] * 4 + [VMEM_SPEC] * 8,
        out_specs=(VMEM_SPEC,) * 4,
        scratch_shapes=work_buffers() + [pltpu.VMEM((VARS, ELEMS, HALF), F32)] * 2,
        compiler_params=params,
    )(
        group_array, species_map, reaction_rate, wave_speed,
        *parts, face_table, fine_volume, coarse_volume, lift_matrix,
    )

    def over(array, other_z, along_x, other_core):
        def place(i, s):
            z, x, core = i // 8, i // 2 % 4, i % 2
            return (z ^ other_z) * 8 + (x + along_x) % 4 * 2 + (core ^ other_core), s

        return sent(array, place)

    low, middle, high = (slice(k * THIRD, (k + 1) * THIRD) for k in range(3))
    below, above, across = over(send, 0, 1, 0), over(send, 0, -1, 0), over(send, 1, 0, 0)
    far_x, across_above, across_below = over(below, 0, 1, 0), over(across, 0, -1, 0), over(below, 1, 0, 0)
    send, below, above, across, far_x, across_above, across_below = lax.optimization_barrier(
        (send, below, above, across, far_x, across_above, across_below)
    )
    last = [
        over(across_above[low], 0, -1, 0),
        over(across_below[middle], 0, 1, 0),
        over(far_x[high], 1, 0, 0),
    ]
    send_pair = over(send, 0, 0, 1)
    below_pair, above_pair, across_pair = (over(item, 0, 0, 1) for item in (below, above, across))
    far_pair, across_above_pair, across_below_pair = (
        over(item, 0, 0, 1) for item in (far_x, across_above, across_below)
    )
    last_pair = [over(item, 0, 0, 1) for item in last]
    terms = [
        send, send_pair, above, above_pair, far_x, far_pair, below, below_pair,
        across, across_pair, across_above, across_above_pair, across_below, across_below_pair,
        *last, *last_pair,
    ]
    out = pl.pallas_call(
        chain_kernel,
        out_shape=jax.ShapeDtypeStruct((STRIDE, VARS, BLOCK, NODES), F32),
        in_specs=[SMEM_SPEC] * 4 + [pl.BlockSpec(memory_space=pl.ANY)] * 20 + [VMEM_SPEC] * 7,
        out_specs=VMEM_SPEC,
        scratch_shapes=work_buffers()
        + [
            pltpu.VMEM((ROWS, NODES), BF),
            pltpu.VMEM((2, ROWS, NODES), BF),
            pltpu.SemaphoreType.DMA((2,)),
        ],
        compiler_params=params,
    )(
        group_array, species_map, reaction_rate, wave_speed,
        *terms, second, base, table, face_table, fine_volume, coarse_volume, lift_matrix,
    )
    return jnp.transpose(out, (0, 2, 1, 3))


def solution(mesh):
    placed = (
        P("tm", "space", None, None),
        P("space", None, None),
        P(),
        P(),
        P(),
        P(),
        P(),
        P(),
        P("space", None),
        P("space", None),
    )
    return jax.shard_map(
        body, mesh=mesh, in_specs=placed, out_specs=P("tm", "space", None, None), check_vma=False
    )
```

```python
import jax
import jax.numpy as jnp
import numpy as np
from jax import lax
from jax.experimental import pallas as pl
from jax.experimental.pallas import tpu as pltpu
from jax.sharding import PartitionSpec as P

SIDE = 8
NODES = 512
FACES = 384
VARS = 12
REACTIONS = 24
BLOCK = 8
BLOCKS = 8
ELEMS = 64
ROWS = VARS * ELEMS
HALF = NODES // 2
PAYLOAD = 112
THIRD = ROWS // 3
OWN = 4
STRIDE = 4
GAIN = 4.0
BF = jnp.bfloat16
F32 = jnp.float32


def swapped_face_table():
    inner = np.arange(64)
    first, second = inner // 8, inner % 8
    nodes = [
        first * 64 + second,
        first * 64 + 56 + second,
        first * 64 + second * 8,
        first * 64 + second * 8 + 7,
    ]
    table = np.zeros((NODES, 256), np.float32)
    for place, face in enumerate((1, 0, 3, 2)):
        table[nodes[face], place * 64 + inner] = 1.0
    return table


def gather_tables(code, table_ref):
    row = lax.broadcasted_iota(jnp.int32, (ELEMS, ELEMS), 0)
    column = lax.broadcasted_iota(jnp.int32, (ELEMS, ELEMS), 1)
    home = row - jnp.bitwise_and(row, 7)
    for pair in range(3):
        parts = []
        for face in (2 * pair, 2 * pair + 1):
            source = jnp.bitwise_and(home + code[:, face : face + 1] + 56, 63)
            parts.append(jnp.where(source == column, 1.0, 0.0))
        table_ref[pair] = jnp.concatenate(parts, axis=1).astype(BF)


def exchange(xj_ref, s_ref, table_ref, face_ref, speed_ref, low, high):
    lane = lax.broadcasted_iota(jnp.int32, (ELEMS, 128), 1)
    left = lane < 64
    zero = jnp.zeros((ELEMS, 128), BF)
    s_ref[:, 128:384] = jnp.dot(
        xj_ref[:, 0:NODES], face_ref[...], preferred_element_type=F32
    ).astype(BF)
    lo = xj_ref[:, 0:128]
    hi = xj_ref[:, NODES - 128 : NODES]
    s_ref[:, 0:128] = jnp.concatenate([hi[:, 64:128], lo[:, 0:64]], axis=1)
    for v in range(0, VARS, 2):
        for pair in range(3):
            lanes = slice(pair * 128, (pair + 1) * 128)
            stacks = []
            for half in range(2):
                swapped = s_ref[(v + half) * ELEMS : (v + half + 1) * ELEMS, lanes]
                stacks.append(
                    jnp.concatenate(
                        [jnp.where(left, swapped, zero), jnp.where(left, zero, swapped)], axis=0
                    )
                )
            across = jnp.dot(
                table_ref[pair, low:high], jnp.concatenate(stacks, axis=1), preferred_element_type=F32
            )
            for half in range(2):
                rows = slice((v + half) * ELEMS + low, (v + half) * ELEMS + high)
                swapped = s_ref[rows, lanes]
                own = jnp.concatenate([swapped[:, 64:128], swapped[:, 0:64]], axis=1).astype(F32)
                xj_ref[rows, NODES + pair * 128 : NODES + (pair + 1) * 128] = (
                    (across[:, half * 128 : (half + 1) * 128] - own) * speed_ref[v + half]
                ).astype(BF)


def move(xj_ref, w_ref, t_ref, cut, row, rows):
    moved = jnp.dot(
        xj_ref[row : row + rows, :],
        w_ref[:, cut * HALF : (cut + 1) * HALF],
        preferred_element_type=F32,
    )
    t_ref[row // ELEMS : (row + rows) // ELEMS] = moved.reshape(rows // ELEMS, ELEMS, HALF)


def move_some(xj_ref, w_ref, t_ref, cut, low, high):
    rows = jnp.concatenate([xj_ref[v * ELEMS + low : v * ELEMS + high, :] for v in range(VARS)], axis=0)
    moved = jnp.dot(
        rows, w_ref[:, cut * HALF : (cut + 1) * HALF], preferred_element_type=F32
    )
    t_ref[:, low:high, :] = moved.reshape(VARS, high - low, HALF)


def prepare(work, cut, low, high):
    rows = slice(low, high)
    t = work.t[cut][:, rows, :]
    work.plus[cut][:, rows, :] = t
    work.square[cut][:, rows, :] = 0.5 + t * t
    work.minus[cut][:, rows, :] = jnp.zeros_like(t)


def react(work, cut, reaction, low, high):
    first, second, made, scale = reaction
    rows = slice(low, high)
    t, square = work.t[cut], work.square[cut]
    rate = scale * (t[first, rows] * t[second, rows]) / (square[first, rows] + square[second, rows])
    work.plus[cut][made, rows] += rate
    work.minus[cut][first, rows] += rate


def result(work, cut, low=0, high=ELEMS):
    return work.plus[cut][:, low:high, :] - work.minus[cut][:, low:high, :]


def own_result(work, cut):
    return result(work, cut, OWN * BLOCK, (OWN + 1) * BLOCK)


def substep(work, reactions, finish):
    exchange(work.xj, work.s, work.table, work.face, work.speed, 0, ELEMS)
    move(work.xj, work.w, work.t[0], 0, 0, ROWS)
    prepare(work, 0, 0, ELEMS)
    for number, reaction in enumerate(reactions):
        react(work, 0, reaction, 0, ELEMS)
        if number % 4 == 1:
            move(work.xj, work.w, work.t[1], 1, number // 4 * 128, 128)
    finish(0)
    prepare(work, 1, 0, ELEMS)
    for reaction in reactions:
        react(work, 1, reaction, 0, ELEMS)
    finish(1)


def substep_some(work, reactions, low, high, store):
    exchange(work.xj, work.s, work.table, work.face, work.speed, low, high)
    for cut in range(2):
        move_some(work.xj, work.w, work.t[cut], cut, low, high)
    for cut in range(2):
        prepare(work, cut, low, high)
        for reaction in reactions:
            react(work, cut, reaction, low, high)
        if store:
            value = result(work, cut, low, high).astype(BF)
            for v in range(VARS):
                work.xj[v * ELEMS + low : v * ELEMS + high, half(cut)] = value[v]


def reactions_of(species_ref, rate_ref, gain):
    return [
        (species_ref[r, 0], species_ref[r, 1], species_ref[r, 2], gain * rate_ref[r])
        for r in range(REACTIONS)
    ]


def half(cut):
    return slice(cut * HALF, (cut + 1) * HALF)


def keep(work):
    def finish(cut):
        work.xj[:, half(cut)] = result(work, cut).astype(BF).reshape(ROWS, HALF)

    return finish


def relax_kernel(group_ref, species_ref, rate_ref, speed_ref, *refs):
    pairs = refs[:4]
    face_ref, fine_ref, coarse_ref, lift_ref = refs[4:8]
    send_ref, base_ref, second_ref, table_ref = refs[8:12]
    work = Work(refs[12:-2], table_ref, face_ref, speed_ref)
    stepped = refs[-2:]
    xj, w = work.xj, work.w
    group = group_ref[0]
    even = group_ref[1] == 0
    near = [pair[0:PAYLOAD].astype(F32) for pair in pairs]
    far = [pair[PAYLOAD:].astype(F32) for pair in pairs]
    values = []
    for k in range(4):
        values += [near[k], jnp.where(even, far[k], far[(k + 1) % 4])]
    for v in range(VARS):
        rows = jnp.concatenate([p[v * BLOCK : (v + 1) * BLOCK] for p in values], axis=0)
        xj[v * ELEMS : (v + 1) * ELEMS, 0:NODES] = rows.astype(BF)
    codes = jnp.concatenate([p[VARS * BLOCK : (VARS + 1) * BLOCK, 0:128] for p in values], axis=0)
    gather_tables(codes.astype(jnp.int32), table_ref)
    w[0:NODES, :] = fine_ref[...]
    w[NODES:, :] = lift_ref[...]
    second_ref[...] = xj[:, 0:NODES]
    reactions = reactions_of(species_ref, rate_ref, 1.0)

    def fine(index, carry):
        substep(work, reactions, keep(work))
        return carry

    lax.fori_loop(0, 8, fine, 0)

    @pl.when(group == 0)
    def _():
        xj[:, 0:NODES] = second_ref[...]

    second_ref[...] = xj[:, 0:NODES]
    w[0:NODES, :] = coarse_ref[...]

    def hold(cut):
        stepped[cut][...] = result(work, cut)

    substep(work, reactions_of(species_ref, rate_ref, GAIN), hold)
    w[0:NODES, :] = fine_ref[...]
    lax.fori_loop(0, 8, fine, 0)
    own = slice(OWN * BLOCK, (OWN + 1) * BLOCK)
    for cut in range(2):
        last = result(work, cut)
        term = last - stepped[cut][...]
        send_ref[:, half(cut)] = jnp.where(group == 1, last, term).astype(BF).reshape(ROWS, HALF)
        base_ref[:, :, half(cut)] = jnp.where(group <= 1, last[:, own], term[:, own])


def chain_kernel(group_ref, species_ref, rate_ref, speed_ref, *refs):
    terms = refs[:20]
    second_ref, base_ref, table_ref, face_ref, fine_ref, coarse_ref, lift_ref, out_ref = refs[20:28]
    work = Work(refs[28:-3], table_ref, face_ref, speed_ref)
    begin, term_buffer, arrived = refs[-3:]
    xj, w = work.xj, work.w
    group = group_ref[0]

    def fetch(item, slot):
        other_z = jnp.bitwise_xor(item, group) & 8
        distance = ((item >> 1) - (group >> 1)) & 3
        place = other_z + 2 * distance + (jnp.bitwise_xor(item, group) & 1)

        def copy(source, rows):
            pltpu.make_async_copy(source, term_buffer.at[slot, rows], arrived.at[slot]).start()

        whole = [n for n in range(16) if n not in (12, 13)]
        for number, n in enumerate(whole):

            @pl.when(place == n)
            def _(number=number):
                copy(terms[number], pl.ds(0, ROWS))

        for n in (12, 13):

            @pl.when(place == n)
            def _(n=n):
                for third in range(3):
                    copy(terms[14 + third + 3 * (n - 12)], pl.ds(third * THIRD, THIRD))

    def await_term(slot):
        pltpu.make_async_copy(terms[0], term_buffer.at[slot], arrived.at[slot]).wait()

    fetch(1, 1)
    w[0:NODES, :] = coarse_ref[...]
    w[NODES:, :] = lift_ref[...]
    begin[...] = second_ref[...]
    out_ref[STRIDE - 1] = base_ref[...]
    await_term(1)
    xj[:, 0:NODES] = term_buffer[1]
    fetch(2, 0)
    coarse_reactions = reactions_of(species_ref, rate_ref, GAIN)

    def chain(index, carry):
        slot = index & 1
        await_term(slot)

        @pl.when(index < 14)
        def _():
            fetch(index + 1, 1 - slot)

        @pl.when(index == group)
        def _():
            begin[...] = xj[:, 0:NODES]

        def chained(cut):
            term = term_buffer[slot, :, half(cut)].astype(F32)
            xj[:, half(cut)] = (result(work, cut).reshape(ROWS, HALF) + term).astype(BF)

        substep(work, coarse_reactions, chained)

        @pl.when(index == group)
        def _():
            for cut in range(2):
                out_ref[STRIDE - 1, :, :, half(cut)] = (
                    own_result(work, cut) + base_ref[:, :, half(cut)]
                )

        return carry

    lax.fori_loop(2, 15, chain, 0)

    @pl.when(group == 15)
    def _():
        begin[...] = xj[:, 0:NODES]
        substep_some(work, coarse_reactions, 32, 48, False)
        for cut in range(2):
            out_ref[STRIDE - 1, :, :, half(cut)] = (
                own_result(work, cut) + base_ref[:, :, half(cut)]
            )

    w[0:NODES, :] = fine_ref[...]
    xj[:, 0:NODES] = begin[...]
    reactions = reactions_of(species_ref, rate_ref, 1.0)

    def fine(number, carry):
        substep(work, reactions, keep(work))

        @pl.when(number == 1)
        def _():
            for cut in range(2):
                out_ref[0, :, :, half(cut)] = own_result(work, cut)

        return carry

    lax.fori_loop(0, 3, fine, 0)
    substep_some(work, reactions, 16, 64, True)
    for cut in range(2):
        out_ref[1, :, :, half(cut)] = own_result(work, cut)
    substep_some(work, reactions, 16, 48, True)
    substep_some(work, reactions, 32, 48, False)
    for cut in range(2):
        out_ref[2, :, :, half(cut)] = own_result(work, cut)


class Work:
    def __init__(self, refs, table, face, speed):
        self.xj, self.s, self.w = refs[:3]
        self.t, self.plus, self.minus, self.square = (refs[i : i + 2] for i in (3, 5, 7, 9))
        self.table, self.face, self.speed = table, face, speed


VMEM_SPEC = pl.BlockSpec(memory_space=pltpu.VMEM)
SMEM_SPEC = pl.BlockSpec(memory_space=pltpu.SMEM)


def work_buffers():
    return [
        pltpu.VMEM((ROWS, NODES + FACES), BF),
        pltpu.VMEM((ROWS, FACES), BF),
        pltpu.VMEM((NODES + FACES, NODES), BF),
    ] + [pltpu.VMEM((VARS, ELEMS, HALF), F32)] * 8


def body(
    coarse_guess,
    initial_state,
    fine_volume,
    coarse_volume,
    lift_matrix,
    wave_speed,
    reaction_rate,
    species_map,
    neighbour_element,
    neighbour_rank,
):
    group = lax.axis_index("tm")
    groups = lax.axis_size("tm")
    start = jnp.where((group == 0) | (group == groups - 1), initial_state, coarse_guess[0])
    start = jnp.transpose(start, (1, 0, 2)).reshape(VARS * BLOCK, NODES).astype(BF)
    code = ((neighbour_rank + 1) * BLOCK + neighbour_element).astype(BF)
    code = jnp.pad(code, ((0, 8), (0, NODES - 6)))
    payload = jnp.concatenate([start, code], axis=0)
    def sent(array, place):
        pairs = []
        for source in range(groups):
            for block in range(BLOCKS):
                target, there = place(source, block)
                pairs.append((source * BLOCKS + block, target % groups * BLOCKS + there % BLOCKS))
        return lax.ppermute(array, ("tm", "space"), pairs)

    near = sent(payload, lambda i, s: (i + 1, s))
    far = sent(payload, lambda i, s: (i + 1, s ^ 1))
    here = jnp.concatenate([near, far], axis=0)
    parts = [
        sent(here, lambda i, s: (i, s + 4)),
        sent(here, lambda i, s: (i, s + 2)),
        here,
        sent(here, lambda i, s: (i, s - 2)),
    ]
    face_table = jnp.asarray(swapped_face_table()).astype(BF)
    group_array = jnp.stack([group, lax.axis_index("space") % 2]).astype(jnp.int32)
    params = pltpu.CompilerParams(vmem_limit_bytes=56 * 1024 * 1024)
    send, base, second, table = pl.pallas_call(
        relax_kernel,
        out_shape=(
            jax.ShapeDtypeStruct((ROWS, NODES), BF),
            jax.ShapeDtypeStruct((VARS, BLOCK, NODES), F32),
            jax.ShapeDtypeStruct((ROWS, NODES), BF),
            jax.ShapeDtypeStruct((3, ELEMS, 128), BF),
        ),
        in_specs=[SMEM_SPEC] * 4 + [VMEM_SPEC] * 8,
        out_specs=(VMEM_SPEC,) * 4,
        scratch_shapes=work_buffers() + [pltpu.VMEM((VARS, ELEMS, HALF), F32)] * 2,
        compiler_params=params,
    )(
        group_array, species_map, reaction_rate, wave_speed,
        *parts, face_table, fine_volume, coarse_volume, lift_matrix,
    )

    def over(array, other_z, along_x, other_core):
        def place(i, s):
            z, x, core = i // 8, i // 2 % 4, i % 2
            return (z ^ other_z) * 8 + (x + along_x) % 4 * 2 + (core ^ other_core), s

        return sent(array, place)

    low, middle, high = (slice(k * THIRD, (k + 1) * THIRD) for k in range(3))
    below, above, across = over(send, 0, 1, 0), over(send, 0, -1, 0), over(send, 1, 0, 0)
    far_x, across_above, across_below = over(below, 0, 1, 0), over(across, 0, -1, 0), over(below, 1, 0, 0)
    held = lax.optimization_barrier((send, below, above, across))
    send_pair, above_pair = over(held[0], 0, 0, 1), over(held[2], 0, 0, 1)
    below, across, far_x, across_above, across_below = lax.optimization_barrier(
        (below, across, far_x, across_above, across_below)
    )
    last = [
        over(across_above[low], 0, -1, 0),
        over(across_below[middle], 0, 1, 0),
        over(far_x[high], 1, 0, 0),
    ]
    below_pair, across_pair = (over(item, 0, 0, 1) for item in (below, across))
    far_pair, across_above_pair, across_below_pair = (
        over(item, 0, 0, 1) for item in (far_x, across_above, across_below)
    )
    last_pair = [over(item, 0, 0, 1) for item in last]
    terms = [
        send, send_pair, above, above_pair, far_x, far_pair, below, below_pair,
        across, across_pair, across_above, across_above_pair, across_below, across_below_pair,
        *last, *last_pair,
    ]
    out = pl.pallas_call(
        chain_kernel,
        out_shape=jax.ShapeDtypeStruct((STRIDE, VARS, BLOCK, NODES), F32),
        in_specs=[SMEM_SPEC] * 4 + [pl.BlockSpec(memory_space=pl.ANY)] * 20 + [VMEM_SPEC] * 7,
        out_specs=VMEM_SPEC,
        scratch_shapes=work_buffers()
        + [
            pltpu.VMEM((ROWS, NODES), BF),
            pltpu.VMEM((2, ROWS, NODES), BF),
            pltpu.SemaphoreType.DMA((2,)),
        ],
        compiler_params=params,
    )(
        group_array, species_map, reaction_rate, wave_speed,
        *terms, second, base, table, face_table, fine_volume, coarse_volume, lift_matrix,
    )
    return jnp.transpose(out, (0, 2, 1, 3))


def solution(mesh):
    placed = (
        P("tm", "space", None, None),
        P("space", None, None),
        P(),
        P(),
        P(),
        P(),
        P(),
        P(),
        P("space", None),
        P("space", None),
    )
    return jax.shard_map(
        body, mesh=mesh, in_specs=placed, out_specs=P("tm", "space", None, None), check_vma=False
    )
```

```python
import jax
import jax.numpy as jnp
import numpy as np
from jax import lax
from jax.experimental import pallas as pl
from jax.experimental.pallas import tpu as pltpu
from jax.sharding import PartitionSpec as P

SIDE = 8
NODES = 512
FACES = 384
VARS = 12
REACTIONS = 24
BLOCK = 8
BLOCKS = 8
ELEMS = 64
ROWS = VARS * ELEMS
HALF = NODES // 2
PAYLOAD = 112
THIRD = ROWS // 3
OWN = 4
STRIDE = 4
GAIN = 4.0
BF = jnp.bfloat16
F32 = jnp.float32


def swapped_face_table():
    inner = np.arange(64)
    first, second = inner // 8, inner % 8
    nodes = [
        first * 64 + second,
        first * 64 + 56 + second,
        first * 64 + second * 8,
        first * 64 + second * 8 + 7,
    ]
    table = np.zeros((NODES, 256), np.float32)
    for place, face in enumerate((1, 0, 3, 2)):
        table[nodes[face], place * 64 + inner] = 1.0
    return table


def gather_tables(code, table_ref):
    row = lax.broadcasted_iota(jnp.int32, (ELEMS, ELEMS), 0)
    column = lax.broadcasted_iota(jnp.int32, (ELEMS, ELEMS), 1)
    home = row - jnp.bitwise_and(row, 7)
    for pair in range(3):
        parts = []
        for face in (2 * pair, 2 * pair + 1):
            source = jnp.bitwise_and(home + code[:, face : face + 1] + 56, 63)
            parts.append(jnp.where(source == column, 1.0, 0.0))
        table_ref[pair] = jnp.concatenate(parts, axis=1).astype(BF)


def exchange(xj_ref, s_ref, table_ref, face_ref, speed_ref, low, high):
    lane = lax.broadcasted_iota(jnp.int32, (ELEMS, 128), 1)
    left = lane < 64
    zero = jnp.zeros((ELEMS, 128), BF)
    s_ref[:, 128:384] = jnp.dot(
        xj_ref[:, 0:NODES], face_ref[...], preferred_element_type=F32
    ).astype(BF)
    lo = xj_ref[:, 0:128]
    hi = xj_ref[:, NODES - 128 : NODES]
    s_ref[:, 0:128] = jnp.concatenate([hi[:, 64:128], lo[:, 0:64]], axis=1)
    for v in range(0, VARS, 2):
        for pair in range(3):
            lanes = slice(pair * 128, (pair + 1) * 128)
            stacks = []
            for half in range(2):
                swapped = s_ref[(v + half) * ELEMS : (v + half + 1) * ELEMS, lanes]
                stacks.append(
                    jnp.concatenate(
                        [jnp.where(left, swapped, zero), jnp.where(left, zero, swapped)], axis=0
                    )
                )
            across = jnp.dot(
                table_ref[pair, low:high], jnp.concatenate(stacks, axis=1), preferred_element_type=F32
            )
            for half in range(2):
                rows = slice((v + half) * ELEMS + low, (v + half) * ELEMS + high)
                swapped = s_ref[rows, lanes]
                own = jnp.concatenate([swapped[:, 64:128], swapped[:, 0:64]], axis=1).astype(F32)
                xj_ref[rows, NODES + pair * 128 : NODES + (pair + 1) * 128] = (
                    (across[:, half * 128 : (half + 1) * 128] - own) * speed_ref[v + half]
                ).astype(BF)


def move(xj_ref, w_ref, t_ref, cut, row, rows):
    moved = jnp.dot(
        xj_ref[row : row + rows, :],
        w_ref[:, cut * HALF : (cut + 1) * HALF],
        preferred_element_type=F32,
    )
    t_ref[row // ELEMS : (row + rows) // ELEMS] = moved.reshape(rows // ELEMS, ELEMS, HALF)


def move_some(xj_ref, w_ref, t_ref, cut, low, high):
    rows = jnp.concatenate([xj_ref[v * ELEMS + low : v * ELEMS + high, :] for v in range(VARS)], axis=0)
    moved = jnp.dot(
        rows, w_ref[:, cut * HALF : (cut + 1) * HALF], preferred_element_type=F32
    )
    t_ref[:, low:high, :] = moved.reshape(VARS, high - low, HALF)


def prepare(work, cut, low, high):
    rows = slice(low, high)
    t = work.t[cut][:, rows, :]
    work.plus[cut][:, rows, :] = t
    work.square[cut][:, rows, :] = 0.5 + t * t
    work.minus[cut][:, rows, :] = jnp.zeros_like(t)


def react(work, cut, reaction, low, high):
    first, second, made, scale = reaction
    rows = slice(low, high)
    t, square = work.t[cut], work.square[cut]
    rate = scale * (t[first, rows] * t[second, rows]) / (square[first, rows] + square[second, rows])
    work.plus[cut][made, rows] += rate
    work.minus[cut][first, rows] += rate


def result(work, cut, low=0, high=ELEMS):
    return work.plus[cut][:, low:high, :] - work.minus[cut][:, low:high, :]


def own_result(work, cut):
    return result(work, cut, OWN * BLOCK, (OWN + 1) * BLOCK)


def substep(work, reactions, finish):
    exchange(work.xj, work.s, work.table, work.face, work.speed, 0, ELEMS)
    move(work.xj, work.w, work.t[0], 0, 0, ROWS)
    prepare(work, 0, 0, ELEMS)
    for number, reaction in enumerate(reactions):
        react(work, 0, reaction, 0, ELEMS)
        if number % 4 == 1:
            move(work.xj, work.w, work.t[1], 1, number // 4 * 128, 128)
    finish(0)
    prepare(work, 1, 0, ELEMS)
    for reaction in reactions:
        react(work, 1, reaction, 0, ELEMS)
    finish(1)


def substep_some(work, reactions, low, high, store):
    exchange(work.xj, work.s, work.table, work.face, work.speed, low, high)
    for cut in range(2):
        move_some(work.xj, work.w, work.t[cut], cut, low, high)
    for cut in range(2):
        prepare(work, cut, low, high)
        for reaction in reactions:
            react(work, cut, reaction, low, high)
        if store:
            value = result(work, cut, low, high).astype(BF)
            for v in range(VARS):
                work.xj[v * ELEMS + low : v * ELEMS + high, half(cut)] = value[v]


def reactions_of(species_ref, rate_ref, gain):
    return [
        (species_ref[r, 0], species_ref[r, 1], species_ref[r, 2], gain * rate_ref[r])
        for r in range(REACTIONS)
    ]


def half(cut):
    return slice(cut * HALF, (cut + 1) * HALF)


def keep(work):
    def finish(cut):
        work.xj[:, half(cut)] = result(work, cut).astype(BF).reshape(ROWS, HALF)

    return finish


def relax_kernel(group_ref, species_ref, rate_ref, speed_ref, *refs):
    pairs = refs[:4]
    face_ref, fine_ref, coarse_ref, lift_ref = refs[4:8]
    send_ref, base_ref, second_ref, table_ref = refs[8:12]
    work = Work(refs[12:-2], table_ref, face_ref, speed_ref)
    stepped = refs[-2:]
    xj, w = work.xj, work.w
    group = group_ref[0]
    even = group_ref[1] == 0
    near = [pair[0:PAYLOAD].astype(F32) for pair in pairs]
    far = [pair[PAYLOAD:].astype(F32) for pair in pairs]
    values = []
    for k in range(4):
        values += [near[k], jnp.where(even, far[k], far[(k + 1) % 4])]
    for v in range(VARS):
        rows = jnp.concatenate([p[v * BLOCK : (v + 1) * BLOCK] for p in values], axis=0)
        xj[v * ELEMS : (v + 1) * ELEMS, 0:NODES] = rows.astype(BF)
    codes = jnp.concatenate([p[VARS * BLOCK : (VARS + 1) * BLOCK, 0:128] for p in values], axis=0)
    gather_tables(codes.astype(jnp.int32), table_ref)
    w[0:NODES, :] = fine_ref[...]
    w[NODES:, :] = lift_ref[...]
    second_ref[...] = xj[:, 0:NODES]
    reactions = reactions_of(species_ref, rate_ref, 1.0)

    def fine(index, carry):
        substep(work, reactions, keep(work))
        return carry

    lax.fori_loop(0, 8, fine, 0)

    @pl.when(group == 0)
    def _():
        xj[:, 0:NODES] = second_ref[...]

    second_ref[...] = xj[:, 0:NODES]
    w[0:NODES, :] = coarse_ref[...]

    def hold(cut):
        stepped[cut][...] = result(work, cut)

    substep(work, reactions_of(species_ref, rate_ref, GAIN), hold)
    w[0:NODES, :] = fine_ref[...]
    lax.fori_loop(0, 8, fine, 0)
    own = slice(OWN * BLOCK, (OWN + 1) * BLOCK)
    for cut in range(2):
        last = result(work, cut)
        term = last - stepped[cut][...]
        send_ref[:, half(cut)] = jnp.where(group == 1, last, term).astype(BF).reshape(ROWS, HALF)
        base_ref[:, :, half(cut)] = jnp.where(group <= 1, last[:, own], term[:, own])


def chain_kernel(group_ref, species_ref, rate_ref, speed_ref, *refs):
    terms = refs[:20]
    second_ref, base_ref, table_ref, face_ref, fine_ref, coarse_ref, lift_ref, out_ref = refs[20:28]
    work = Work(refs[28:-3], table_ref, face_ref, speed_ref)
    begin, term_buffer, arrived = refs[-3:]
    xj, w = work.xj, work.w
    group = group_ref[0]

    def fetch(item, slot):
        other_z = jnp.bitwise_xor(item, group) & 8
        distance = ((item >> 1) - (group >> 1)) & 3
        place = other_z + 2 * distance + (jnp.bitwise_xor(item, group) & 1)

        def copy(source, rows):
            pltpu.make_async_copy(source, term_buffer.at[slot, rows], arrived.at[slot]).start()

        whole = [n for n in range(16) if n not in (12, 13)]
        for number, n in enumerate(whole):

            @pl.when(place == n)
            def _(number=number):
                copy(terms[number], pl.ds(0, ROWS))

        for n in (12, 13):

            @pl.when(place == n)
            def _(n=n):
                for third in range(3):
                    copy(terms[14 + third + 3 * (n - 12)], pl.ds(third * THIRD, THIRD))

    def await_term(slot):
        pltpu.make_async_copy(terms[0], term_buffer.at[slot], arrived.at[slot]).wait()

    fetch(1, 1)
    w[0:NODES, :] = coarse_ref[...]
    w[NODES:, :] = lift_ref[...]
    begin[...] = second_ref[...]
    out_ref[STRIDE - 1] = base_ref[...]
    await_term(1)
    xj[:, 0:NODES] = term_buffer[1]
    fetch(2, 0)
    coarse_reactions = reactions_of(species_ref, rate_ref, GAIN)

    def chain(index, carry):
        slot = index & 1
        await_term(slot)

        @pl.when(index < 14)
        def _():
            fetch(index + 1, 1 - slot)

        @pl.when(index == group)
        def _():
            begin[...] = xj[:, 0:NODES]

        def chained(cut):
            term = term_buffer[slot, :, half(cut)].astype(F32)
            xj[:, half(cut)] = (result(work, cut).reshape(ROWS, HALF) + term).astype(BF)

        substep(work, coarse_reactions, chained)

        @pl.when(index == group)
        def _():
            for cut in range(2):
                out_ref[STRIDE - 1, :, :, half(cut)] = (
                    own_result(work, cut) + base_ref[:, :, half(cut)]
                )

        return carry

    lax.fori_loop(2, 15, chain, 0)

    @pl.when(group == 15)
    def _():
        begin[...] = xj[:, 0:NODES]
        substep_some(work, coarse_reactions, 32, 48, False)
        for cut in range(2):
            out_ref[STRIDE - 1, :, :, half(cut)] = (
                own_result(work, cut) + base_ref[:, :, half(cut)]
            )

    w[0:NODES, :] = fine_ref[...]
    xj[:, 0:NODES] = begin[...]
    reactions = reactions_of(species_ref, rate_ref, 1.0)

    def fine(number, carry):
        substep(work, reactions, keep(work))

        @pl.when(number == 1)
        def _():
            for cut in range(2):
                out_ref[0, :, :, half(cut)] = own_result(work, cut)

        return carry

    lax.fori_loop(0, 3, fine, 0)
    substep_some(work, reactions, 16, 64, True)
    for cut in range(2):
        out_ref[1, :, :, half(cut)] = own_result(work, cut)
    substep_some(work, reactions, 16, 48, True)
    substep_some(work, reactions, 32, 48, False)
    for cut in range(2):
        out_ref[2, :, :, half(cut)] = own_result(work, cut)


class Work:
    def __init__(self, refs, table, face, speed):
        self.xj, self.s, self.w = refs[:3]
        self.t, self.plus, self.minus, self.square = (refs[i : i + 2] for i in (3, 5, 7, 9))
        self.table, self.face, self.speed = table, face, speed


VMEM_SPEC = pl.BlockSpec(memory_space=pltpu.VMEM)
SMEM_SPEC = pl.BlockSpec(memory_space=pltpu.SMEM)


def work_buffers():
    return [
        pltpu.VMEM((ROWS, NODES + FACES), BF),
        pltpu.VMEM((ROWS, FACES), BF),
        pltpu.VMEM((NODES + FACES, NODES), BF),
    ] + [pltpu.VMEM((VARS, ELEMS, HALF), F32)] * 8


def body(
    coarse_guess,
    initial_state,
    fine_volume,
    coarse_volume,
    lift_matrix,
    wave_speed,
    reaction_rate,
    species_map,
    neighbour_element,
    neighbour_rank,
):
    group = lax.axis_index("tm")
    groups = lax.axis_size("tm")
    start = jnp.where((group == 0) | (group == groups - 1), initial_state, coarse_guess[0])
    start = jnp.transpose(start, (1, 0, 2)).reshape(VARS * BLOCK, NODES).astype(BF)
    code = ((neighbour_rank + 1) * BLOCK + neighbour_element).astype(BF)
    code = jnp.pad(code, ((0, 8), (0, NODES - 6)))
    payload = jnp.concatenate([start, code], axis=0)
    def sent(array, place):
        pairs = []
        for source in range(groups):
            for block in range(BLOCKS):
                target, there = place(source, block)
                pairs.append((source * BLOCKS + block, target % groups * BLOCKS + there % BLOCKS))
        return lax.ppermute(array, ("tm", "space"), pairs)

    near = sent(payload, lambda i, s: (i + 1, s))
    far = sent(payload, lambda i, s: (i + 1, s ^ 1))
    here = jnp.concatenate([near, far], axis=0)
    parts = [
        sent(here, lambda i, s: (i, s + 4)),
        sent(here, lambda i, s: (i, s + 2)),
        here,
        sent(here, lambda i, s: (i, s - 2)),
    ]
    face_table = jnp.asarray(swapped_face_table()).astype(BF)
    group_array = jnp.stack([group, lax.axis_index("space") % 2]).astype(jnp.int32)
    params = pltpu.CompilerParams(vmem_limit_bytes=56 * 1024 * 1024)
    send, base, second, table = pl.pallas_call(
        relax_kernel,
        out_shape=(
            jax.ShapeDtypeStruct((ROWS, NODES), BF),
            jax.ShapeDtypeStruct((VARS, BLOCK, NODES), F32),
            jax.ShapeDtypeStruct((ROWS, NODES), BF),
            jax.ShapeDtypeStruct((3, ELEMS, 128), BF),
        ),
        in_specs=[SMEM_SPEC] * 4 + [VMEM_SPEC] * 8,
        out_specs=(VMEM_SPEC,) * 4,
        scratch_shapes=work_buffers() + [pltpu.VMEM((VARS, ELEMS, HALF), F32)] * 2,
        compiler_params=params,
    )(
        group_array, species_map, reaction_rate, wave_speed,
        *parts, face_table, fine_volume, coarse_volume, lift_matrix,
    )

    def over(array, other_z, along_x, other_core):
        def place(i, s):
            z, x, core = i // 8, i // 2 % 4, i % 2
            return (z ^ other_z) * 8 + (x + along_x) % 4 * 2 + (core ^ other_core), s

        return sent(array, place)

    low, middle, high = (slice(k * THIRD, (k + 1) * THIRD) for k in range(3))
    below, above, across = over(send, 0, 1, 0), over(send, 0, -1, 0), over(send, 1, 0, 0)
    far_x, across_above, across_below = over(below, 0, 1, 0), over(across, 0, -1, 0), over(below, 1, 0, 0)
    held = lax.optimization_barrier((send, below, above, across))
    send_pair, above_pair = over(held[0], 0, 0, 1), over(held[2], 0, 0, 1)
    after = lax.optimization_barrier((send_pair, above_pair, below, across))
    below_pair, across_pair = over(after[2], 0, 0, 1), over(after[3], 0, 0, 1)
    below_pair, across_pair, far_x, across_above, across_below = lax.optimization_barrier(
        (below_pair, across_pair, far_x, across_above, across_below)
    )
    last = [
        over(across_above[low], 0, -1, 0),
        over(across_below[middle], 0, 1, 0),
        over(far_x[high], 1, 0, 0),
    ]
    *last, far_x, across_above, across_below = lax.optimization_barrier(
        (*last, far_x, across_above, across_below)
    )
    far_pair, across_above_pair, across_below_pair = (
        over(item, 0, 0, 1) for item in (far_x, across_above, across_below)
    )
    last_pair = [over(item, 0, 0, 1) for item in last]
    terms = [
        send, send_pair, above, above_pair, far_x, far_pair, below, below_pair,
        across, across_pair, across_above, across_above_pair, across_below, across_below_pair,
        *last, *last_pair,
    ]
    out = pl.pallas_call(
        chain_kernel,
        out_shape=jax.ShapeDtypeStruct((STRIDE, VARS, BLOCK, NODES), F32),
        in_specs=[SMEM_SPEC] * 4 + [pl.BlockSpec(memory_space=pl.ANY)] * 20 + [VMEM_SPEC] * 7,
        out_specs=VMEM_SPEC,
        scratch_shapes=work_buffers()
        + [
            pltpu.VMEM((ROWS, NODES), BF),
            pltpu.VMEM((2, ROWS, NODES), BF),
            pltpu.SemaphoreType.DMA((2,)),
        ],
        compiler_params=params,
    )(
        group_array, species_map, reaction_rate, wave_speed,
        *terms, second, base, table, face_table, fine_volume, coarse_volume, lift_matrix,
    )
    return jnp.transpose(out, (0, 2, 1, 3))


def solution(mesh):
    placed = (
        P("tm", "space", None, None),
        P("space", None, None),
        P(),
        P(),
        P(),
        P(),
        P(),
        P(),
        P("space", None),
        P("space", None),
    )
    return jax.shard_map(
        body, mesh=mesh, in_specs=placed, out_specs=P("tm", "space", None, None), check_vma=False
    )
```
